512 devices in a mesh: field: 32 (over x, y_lo, core), slab: 16 (over y_hi, z).
Axes of the slice: x: 4, y: 8 (y_hi: 2, y_lo: 4; y = y_hi * 4 + y_lo), z: 8, core: 2. Of those that a mesh axis runs over, the one named last changes fastest.
Arguments:
- fields: float32 [32, 16, 64, 16, 128], P('field', None, 'slab'), may hold values from -6 to 6
- velocity: float32 [3, 64, 16, 128], P(None, 'slab'), may hold values from -0.15 to 0.15
- diffusivity: float32 [64, 16, 128], P('slab'), may hold values from 0.06 to 0.14
- noise: float32 [32, 4, 3], P('field'), may hold values from -0.8 to 0.8
- mix_rate: float32 [64, 16, 128], P('slab'), may hold values from 0.2 to 1
- evaporation: float32 [64, 16, 128], P('slab'), may hold values from 0.05 to 0.5
- rate_matrix: float32 [32, 16], replicated, may hold values from -1.5 to 1.5
- stoich: float32 [16, 32], replicated, may hold values from -1 to 1
- prefactor: float32 [32], replicated, may hold values from 0.05 to 0.5
Outputs:
- updated: float32 [32, 16, 64, 16, 128], P('field', None, 'slab')
The draws below stay inside these ranges and needn't reach their ends.
All inputs are finite; a program needn't handle non-finite values.
Results may differ from the reference program's by a relative error of at most 0.000073.
Values sent between devices are 32-bit elements; how exact they have to be, the bound alone decides.
No kernel may reach another device: no remote copies, remote signals or barrier semaphores. Data moves between devices by JAX's collectives and lax.ppermute only.
A program may use at most 64 MiB of HBM per device.

```python
import math
import jax
import jax.numpy as jnp
from jax import lax

F = 32
S = 16
R = 32
SUBSTEPS = 4
NZ = 16
NY = 128
NX = 64


def levels(stream_key, extent, shards, least, top_value):
    factor_of = 1.0
    for position, shards_of in shards:
        heights = jax.random.uniform(jax.random.fold_in(jax.random.fold_in(stream_key, 6), position), (shards_of,), jnp.float32, least / len(shards), top_value / len(shards))
        factor_of = factor_of * jnp.repeat(jnp.exp(heights), extent[position] // shards_of).reshape((-1,) + (1,) * (len(extent) - 1 - position))
    return factor_of


def centred(stream_key, extent, scale, reach, split=(), kind=jnp.bfloat16):
    entries = scale * jax.random.normal(stream_key, extent, jnp.float32)
    if split:
        entries = entries * levels(stream_key, extent, split, -0.22, 0.18)
    return jnp.clip(entries, -reach, reach).astype(kind)


def setup_inputs(seed: int = 0) -> dict:
    key_of = jax.random.split(jax.random.key(seed), 10)
    fields = centred(key_of[0], (F, S, NX, NZ, NY), 1.0, 6.0, ((0, 32), (2, 16)), jnp.float32)
    velocity = jnp.clip(jax.random.uniform(key_of[1], (3, NX, NZ, NY), jnp.float32, -0.15, 0.15) * levels(key_of[1], (3, NX, NZ, NY), ((1, 16),), -0.4, 0.0), -0.15, 0.15)
    diffusivity = jnp.clip(0.06 + 0.08 * jax.random.uniform(key_of[2], (NX, NZ, NY), jnp.float32) ** levels(key_of[2], (NX, NZ, NY), ((0, 16),), -0.2, 0.2), 0.06, 0.14)
    noise = centred(key_of[3], (F, SUBSTEPS, 3), 0.2, 0.8, ((0, 32),), jnp.float32)
    mix_rate = jnp.clip(jnp.exp(math.log(1.0) - 1.609438 * jax.random.uniform(key_of[4], (NX, NZ, NY), jnp.float32) ** levels(key_of[4], (NX, NZ, NY), ((0, 16),), -0.2, 0.2)), 0.2, 1.0)
    evaporation = jnp.clip(jnp.exp(math.log(0.5) - 2.3025851 * jax.random.uniform(key_of[5], (NX, NZ, NY), jnp.float32) ** levels(key_of[5], (NX, NZ, NY), ((0, 16),), -0.2, 0.2)), 0.05, 0.5)
    rate_matrix = centred(key_of[6], (R, S), S ** -0.5, 1.5, (), jnp.float32)
    stoich = centred(key_of[7], (S, R), R ** -0.5, 1.0, (), jnp.float32)
    prefactor = jnp.clip(jnp.exp(jax.random.uniform(key_of[8], (R,), jnp.float32, math.log(0.05), math.log(0.5))), 0.05, 0.5)
    return dict(fields=fields, velocity=velocity, diffusivity=diffusivity, noise=noise, mix_rate=mix_rate, evaporation=evaporation, rate_matrix=rate_matrix, stoich=stoich, prefactor=prefactor)


def advance(padded, velocity, diffusivity, drifts):
    center = padded[:, :, 1:-1]
    x_ahead = padded[:, :, 2:]
    x_behind = padded[:, :, :-2]
    y_ahead = jnp.roll(center, -1, axis=4)
    y_behind = jnp.roll(center, 1, axis=4)
    z_ahead = jnp.roll(center, -1, axis=3)
    z_behind = jnp.roll(center, 1, axis=3)
    spread = x_ahead + x_behind + y_ahead + y_behind + z_ahead + z_behind - 6.0 * center
    stir_scale = jnp.sqrt(2.0 * diffusivity)
    drift_x = velocity[0] - stir_scale * drifts[:, 0][:, None, None, None, None]
    drift_y = velocity[1] - stir_scale * drifts[:, 1][:, None, None, None, None]
    drift_z = velocity[2] - stir_scale * drifts[:, 2][:, None, None, None, None]
    carried = drift_x * (x_ahead - x_behind) * 0.5 + drift_y * (y_ahead - y_behind) * 0.5 + drift_z * (z_ahead - z_behind) * 0.5
    return center + diffusivity * spread - carried

def react(states, average, rates, vapour, rate_matrix, stoich, prefactor):
    species = states.shape[1]
    fuel = (jnp.arange(species) == 0).astype(jnp.float32)
    mixed = states - 0.5 * rates * (states - average) + vapour * fuel[:, None]
    drive = jnp.einsum('rs,ksc->krc', rate_matrix, mixed, precision=lax.Precision.HIGHEST)
    speed = prefactor[None, :, None] * jnp.exp(2.0 * jnp.tanh(drive))
    return mixed + jnp.einsum('sr,krc->ksc', stoich, speed, precision=lax.Precision.HIGHEST)

def reference(fields, velocity, diffusivity, noise, mix_rate, evaporation, rate_matrix, stoich, prefactor):

    def carry_field(packed):
        state, drifts = packed
        state = state[None]
        for substep in range(SUBSTEPS):
            padded = jnp.pad(state, ((0, 0), (0, 0), (1, 1), (0, 0), (0, 0)))
            state = advance(padded, velocity, diffusivity, drifts[substep][None])
        return state[0]
    moved = lax.map(carry_field, (fields, noise))
    average = (lax.optimization_barrier(jnp.sum(moved, axis=0)) / F).reshape(S, -1)
    rates = mix_rate.reshape(-1)
    vapour = evaporation.reshape(-1)

    def react_field(state):
        result = react(state.reshape(1, S, -1), average, rates, vapour, rate_matrix, stoich, prefactor)
        return result[0].reshape(state.shape)
    return lax.map(react_field, moved)
```

```python
import functools

import jax
import jax.numpy as jnp
from jax import lax
from jax.experimental import pallas as pl
from jax.experimental.pallas import tpu as pltpu
from jax.sharding import Mesh
from jax.sharding import PartitionSpec as P

F = 32
S = 16
R = 32
SUBSTEPS = 4
X = 4
NZ = 16
NY = 128
HALF = S // 2
CHIPS = ("field_0", "field_1")
FIELD = ("field_0", "field_1", "field_2")


def transport_kernel(core_ref, noise_ref, own_ref, prev_ref, next_ref, moved_ref, keep_ref, send_ref, coef_ref):
    core = core_ref[0]

    def layer(channel, i):
        ref, j = (prev_ref, i) if i < X else (own_ref, i - X) if i < 2 * X else (next_ref, i - 2 * X)
        return ref[channel, j]

    slot = 0
    slots = {}
    for i in range(1, 3 * X - 1):
        diff = layer(S + 3, i)
        vx, vy, vz = layer(S, i), layer(S + 1, i), layer(S + 2, i)
        stir = jnp.sqrt(2.0 * diff)
        center = 1.0 - 6.0 * diff
        for k in range(SUBSTEPS):
            if not k < i < 3 * X - 1 - k:
                continue
            slots[k, i] = slot
            hx = 0.5 * (vx - stir * noise_ref[3 * k])
            hy = 0.5 * (vy - stir * noise_ref[3 * k + 1])
            hz = 0.5 * (vz - stir * noise_ref[3 * k + 2])
            for n, c in enumerate((center, diff - hx, diff + hx, diff - hy, diff + hy, diff - hz, diff + hz)):
                coef_ref[slot, n] = c
            slot += 1

    def one(s, carry):
        state = [layer(s, i) for i in range(3 * X)]
        for k in range(SUBSTEPS):
            new = [None] * (3 * X)
            for i in range(k + 1, 3 * X - 1 - k):
                c = coef_ref.at[slots[k, i]]
                mid = state[i]
                new[i] = (
                    c[0] * mid
                    + c[1] * state[i + 1]
                    + c[2] * state[i - 1]
                    + c[3] * pltpu.roll(mid, NY - 1, 1)
                    + c[4] * pltpu.roll(mid, 1, 1)
                    + c[5] * pltpu.roll(mid, NZ - 1, 0)
                    + c[6] * pltpu.roll(mid, 1, 0)
                )
            state = new
        out = jnp.stack(state[X : 2 * X])
        moved_ref[s] = out
        mine = s // HALF == core

        @pl.when(mine)
        def _():
            keep_ref[s % HALF] = out

        @pl.when(jnp.logical_not(mine))
        def _():
            send_ref[s % HALF] = out

        return carry

    lax.fori_loop(0, S, one, 0)


def transport(core, noise, own, prev, following):
    half = jax.ShapeDtypeStruct((HALF, X, NZ, NY), jnp.float32)
    vmem = pl.BlockSpec(memory_space=pltpu.VMEM)
    smem = pl.BlockSpec(memory_space=pltpu.SMEM)
    return pl.pallas_call(
        transport_kernel,
        out_shape=(jax.ShapeDtypeStruct((S, X, NZ, NY), jnp.float32), half, half),
        in_specs=[smem, smem, vmem, vmem, vmem],
        out_specs=(vmem, vmem, vmem),
        scratch_shapes=[pltpu.VMEM((28, 7, NZ, NY), jnp.float32)],
        compiler_params=pltpu.CompilerParams(vmem_limit_bytes=32 * 2**20),
        name="transport",
    )(core, noise, own, prev, following)


def halves(x):
    hi = x.astype(jnp.bfloat16)
    return hi, (x - hi.astype(jnp.float32)).astype(jnp.bfloat16)


def product(weights, values):
    whi, wlo = weights
    vhi, vlo = halves(values)
    return lax.dot_general(
        jnp.concatenate([whi, whi, wlo], 0),
        jnp.concatenate([vhi, vlo, vhi], 0),
        (((0,), (0,)), ((), ())),
        preferred_element_type=jnp.float32,
    )


ROWS = 2


def react_kernel(core_ref, moved_ref, mine_ref, other_ref, rate_ref, vapour_ref, rate_matrix_ref, stoich_ref, out_ref):
    cells = X * NZ
    drive_weights = halves(rate_matrix_ref[...])
    source_weights = halves(stoich_ref[...])
    first = core_ref[0] == 0
    fuel = lax.broadcasted_iota(jnp.int32, (S, NY), 0) == 0

    def one(step, carry):
        mixed = []
        for j in range(ROWS):
            r = step * ROWS + j
            moved = moved_ref[pl.ds(r, S, stride=cells), :]
            mine = mine_ref[pl.ds(r, HALF, stride=cells), :]
            other = other_ref[pl.ds(r, HALF, stride=cells), :]
            average = jnp.concatenate([jnp.where(first, mine, other), jnp.where(first, other, mine)], 0)
            rate = rate_ref[pl.ds(r, 1), :]
            vapour = vapour_ref[pl.ds(r, 1), :]
            mixed.append(moved - 0.5 * rate * (moved - average) + jnp.where(fuel, vapour, 0.0))
        mixed = jnp.concatenate(mixed, 1)
        drive = product(drive_weights, mixed)
        speed = jnp.exp(2.0 * jnp.tanh(drive))
        updated = mixed + product(source_weights, speed)
        for j in range(ROWS):
            out_ref[pl.ds(step * ROWS + j, S, stride=cells), :] = updated[:, j * NY : (j + 1) * NY]
        return carry

    lax.fori_loop(0, cells // ROWS, one, 0)


def react(core, moved, mine, other, rates, vapour, rate_matrix, stoich, prefactor):
    vmem = pl.BlockSpec(memory_space=pltpu.VMEM)
    smem = pl.BlockSpec(memory_space=pltpu.SMEM)
    rows = X * NZ
    return pl.pallas_call(
        react_kernel,
        out_shape=jax.ShapeDtypeStruct((S * rows, NY), jnp.float32),
        in_specs=[smem] + [vmem] * 7,
        out_specs=vmem,
        compiler_params=pltpu.CompilerParams(vmem_limit_bytes=32 * 2**20),
        name="react",
    )(
        core,
        moved.reshape(S * rows, NY),
        mine.reshape(HALF * rows, NY),
        other.reshape(HALF * rows, NY),
        rates.reshape(rows, NY),
        vapour.reshape(rows, NY),
        rate_matrix.T,
        (stoich * prefactor[None]).T,
    )


def per_device(fields, velocity, diffusivity, noise, mix_rate, evaporation, rate_matrix, stoich, prefactor):
    slabs = lax.axis_size("slab")
    core = lax.axis_index("field_2").astype(jnp.int32)[None]
    own = jnp.concatenate([fields[0], velocity, diffusivity[None]], 0)
    prev = lax.ppermute(own, "slab", [(i, i + 1) for i in range(slabs - 1)])
    following = lax.ppermute(own, "slab", [(i + 1, i) for i in range(slabs - 1)])
    moved, keep, send = transport(core, noise.reshape(-1), own, prev, following)
    swap = functools.partial(lax.ppermute, axis_name="field_2", perm=[(0, 1), (1, 0)])
    chips = lax.axis_size(CHIPS)
    pair = (keep + swap(send)).reshape(chips, -1, NZ, NY)
    parts = lax.all_to_all(pair, CHIPS, 0, 0, tiled=True)
    average = jnp.sum(parts, 0) / F
    spread = jnp.broadcast_to(average[None], pair.shape)
    mine = lax.all_to_all(spread, CHIPS, 0, 0, tiled=True)
    updated = react(core, moved, mine, swap(mine), mix_rate, evaporation, rate_matrix, stoich, prefactor)
    return updated.reshape(fields.shape)


def solution(mesh):
    split = Mesh(mesh.devices.reshape(4, 4, 2, mesh.shape["slab"]), (*FIELD, "slab"))
    return jax.shard_map(
        per_device,
        mesh=split,
        in_specs=(
            P(FIELD, None, "slab", None, None),
            P(None, "slab", None, None),
            P("slab", None, None),
            P(FIELD, None, None),
            P("slab", None, None),
            P("slab", None, None),
            P(),
            P(),
            P(),
        ),
        out_specs=P(FIELD, None, "slab", None, None),
        check_vma=False,
    )
```

```python
import functools

import jax
import jax.numpy as jnp
from jax import lax
from jax.experimental import pallas as pl
from jax.experimental.pallas import tpu as pltpu
from jax.sharding import Mesh
from jax.sharding import PartitionSpec as P

F = 32
S = 16
R = 32
SUBSTEPS = 4
X = 4
NZ = 16
NY = 128
HALF = S // 2
SEAM = 7
CHIPS = ("field_0", "field_1")
FIELD = ("field_0", "field_1", "field_2")


SLOT = {}
for _i in range(1, 3 * X - 1):
    for _k in range(SUBSTEPS):
        if _k < _i < 3 * X - 1 - _k:
            SLOT[_k, _i] = len(SLOT)
TOGETHER = 4
VMEM = pl.BlockSpec(memory_space=pltpu.VMEM)
SMEM = pl.BlockSpec(memory_space=pltpu.SMEM)
LIMIT = pltpu.CompilerParams(vmem_limit_bytes=48 * 2**20)


def pack_kernel(where_ref, fields_ref, velocity_ref, diffusivity_ref, sent_ref, kept_ref, sems):
    core = where_ref[0]
    copies = [
        pltpu.make_async_copy(fields_ref.at[0, pl.ds((1 - core) * HALF, HALF)], sent_ref.at[pl.ds(0, HALF)], sems.at[0]),
        pltpu.make_async_copy(velocity_ref, sent_ref.at[pl.ds(HALF, 3)], sems.at[1]),
        pltpu.make_async_copy(diffusivity_ref, sent_ref.at[HALF + 3], sems.at[2]),
        pltpu.make_async_copy(fields_ref.at[0, pl.ds(core * HALF, HALF)], kept_ref, sems.at[3]),
    ]
    for c in copies:
        c.start()
    for c in copies:
        c.wait()


def pack(where, fields, velocity, diffusivity):
    return pl.pallas_call(
        pack_kernel,
        out_shape=(
            jax.ShapeDtypeStruct((HALF + 4, X, NZ, NY), jnp.float32),
            jax.ShapeDtypeStruct((HALF, X, NZ, NY), jnp.float32),
        ),
        in_specs=[SMEM] + [pl.BlockSpec(memory_space=pltpu.HBM)] * 3,
        out_specs=(VMEM, VMEM),
        scratch_shapes=[pltpu.SemaphoreType.DMA((4,))],
        compiler_params=LIMIT,
        name="pack",
    )(where, fields, velocity, diffusivity)


def coefficients(noise_ref, layer, coef_ref):
    for i in range(1, 3 * X - 1):
        diff = layer(HALF + 3, i)
        vx, vy, vz = layer(HALF, i), layer(HALF + 1, i), layer(HALF + 2, i)
        stir = jnp.sqrt(2.0 * diff)
        center = 1.0 - 6.0 * diff
        for k in range(SUBSTEPS):
            if (k, i) not in SLOT:
                continue
            hx = 0.5 * (vx - stir * noise_ref[k, 0])
            hy = 0.5 * (vy - stir * noise_ref[k, 1])
            hz = 0.5 * (vz - stir * noise_ref[k, 2])
            for n, c in enumerate((center, diff - hx, diff + hx, diff - hy, diff + hy, diff - hz, diff + hz)):
                coef_ref[SLOT[k, i], n] = c


def substeps(layer, coef_ref, out_ref):
    def some(g, carry):
        scalars = pl.ds(g * TOGETHER, TOGETHER)
        state = [layer(scalars, i) for i in range(3 * X)]
        for k in range(SUBSTEPS):
            new = [None] * (3 * X)
            for i in range(k + 1, 3 * X - 1 - k):
                c = coef_ref.at[SLOT[k, i]]
                mid = state[i]
                new[i] = (
                    (c[0][None] * mid + c[1][None] * state[i + 1] + c[2][None] * state[i - 1])
                    + (c[3][None] * pltpu.roll(mid, NY - 1, 2) + c[4][None] * pltpu.roll(mid, 1, 2))
                    + (c[5][None] * pltpu.roll(mid, NZ - 1, 1) + c[6][None] * pltpu.roll(mid, 1, 1))
                )
            state = new
        for j in range(X):
            out_ref[scalars, j] = state[X + j]
        return carry

    lax.fori_loop(0, HALF // TOGETHER, some, 0)


def sent_kernel(noise_ref, own_ref, prev_ref, next_ref, out_ref, coef_ref):
    def layer(channel, i):
        ref, j = (prev_ref, i) if i < X else (own_ref, i - X) if i < 2 * X else (next_ref, i - 2 * X)
        return ref[channel, j]

    coefficients(noise_ref, layer, coef_ref)
    substeps(layer, coef_ref, out_ref)


def transport_sent(noise, own, prev, following):
    return pl.pallas_call(
        sent_kernel,
        out_shape=(
            jax.ShapeDtypeStruct((HALF, X, NZ, NY), jnp.float32),
            jax.ShapeDtypeStruct((len(SLOT), 7, NZ, NY), jnp.float32),
        ),
        in_specs=[SMEM, VMEM, VMEM, VMEM],
        out_specs=(VMEM, VMEM),
        compiler_params=LIMIT,
        name="transport_sent",
    )(noise, own, prev, following)


def kept_kernel(where_ref, own_ref, prev_ref, next_ref, crossed_ref, coef_ref, out_ref):
    low = where_ref[1] == SEAM
    high = where_ref[1] == SEAM + 1

    def layer(channel, i):
        if i < X:
            return jnp.where(high, crossed_ref[channel, i], prev_ref[channel, i])
        if i < 2 * X:
            return own_ref[channel, i - X]
        return jnp.where(low, crossed_ref[channel, i - 2 * X], next_ref[channel, i - 2 * X])

    substeps(layer, coef_ref, out_ref)


def transport_kept(where, own, prev, following, crossed, coef):
    return pl.pallas_call(
        kept_kernel,
        out_shape=jax.ShapeDtypeStruct((HALF, X, NZ, NY), jnp.float32),
        in_specs=[SMEM] + [VMEM] * 5,
        out_specs=VMEM,
        compiler_params=LIMIT,
        name="transport_kept",
    )(where, own, prev, following, crossed, coef)


def halves(x):
    hi = x.astype(jnp.bfloat16)
    return hi, (x - hi.astype(jnp.float32)).astype(jnp.bfloat16)


def product(weights, values):
    whi, wlo = weights
    vhi, vlo = halves(values)
    return lax.dot_general(
        jnp.concatenate([whi, whi, wlo], 0),
        jnp.concatenate([vhi, vlo, vhi], 0),
        (((0,), (0,)), ((), ())),
        preferred_element_type=jnp.float32,
    )


ROWS = 16


def react_kernel(
    where_ref, sent_ref, kept_ref, mine_ref, other_ref, rate_ref, vapour_ref, rate_matrix_ref, stoich_ref, out_ref
):
    cells = X * NZ
    drive_weights = halves(rate_matrix_ref[...])
    source_weights = halves(stoich_ref[...])
    first = where_ref[0] == 0
    fuel = lax.broadcasted_iota(jnp.int32, (S, NY), 0) == 0

    def some(step, carry):
        mixed = []
        for j in range(ROWS):
            r = step * ROWS + j
            sent, kept, mine, other = (
                ref[pl.ds(r, HALF, stride=cells), :] for ref in (sent_ref, kept_ref, mine_ref, other_ref)
            )
            rate = 0.5 * rate_ref[pl.ds(r, 1), :]
            vapour = vapour_ref[pl.ds(r, 1), :]
            kept = kept - rate * (kept - mine)
            sent = sent - rate * (sent - other)
            both = jnp.concatenate([jnp.where(first, kept, sent), jnp.where(first, sent, kept)], 0)
            mixed.append(both + jnp.where(fuel, vapour, 0.0))
        mixed = jnp.concatenate(mixed, 1)
        speed = jnp.exp(2.0 * jnp.tanh(product(drive_weights, mixed)))
        updated = mixed + product(source_weights, speed)
        for j in range(ROWS):
            out_ref[pl.ds(step * ROWS + j, S, stride=cells), :] = updated[:, j * NY : (j + 1) * NY]
        return carry

    lax.fori_loop(0, cells // ROWS, some, 0, unroll=2)


def react(where, sent, kept, mine, other, rates, vapour, rate_matrix, stoich, prefactor):
    rows = X * NZ
    return pl.pallas_call(
        react_kernel,
        out_shape=jax.ShapeDtypeStruct((S * rows, NY), jnp.float32),
        in_specs=[SMEM] + [VMEM] * 8,
        out_specs=VMEM,
        compiler_params=LIMIT,
        name="react",
    )(
        where,
        *(x.reshape(HALF * rows, NY) for x in (sent, kept, mine, other)),
        rates.reshape(rows, NY),
        vapour.reshape(rows, NY),
        rate_matrix.T,
        (stoich * prefactor[None]).T,
    )


def per_device(fields, velocity, diffusivity, noise, mix_rate, evaporation, rate_matrix, stoich, prefactor):
    slabs = lax.axis_size("slab")
    where = jnp.stack([lax.axis_index("field_2"), lax.axis_index("slab")]).astype(jnp.int32)
    up = [(i, i + 1) for i in range(slabs - 1)]
    down = [(i + 1, i) for i in range(slabs - 1)]
    send, keep = pack(where, fields, velocity, diffusivity)
    send_prev = lax.ppermute(send, "slab", up)
    send_next = lax.ppermute(send, "slab", down)
    halfway = lax.ppermute(keep, "slab", [(SEAM, slabs - 1), (SEAM + 1, 0)])
    crossed = lax.ppermute(halfway, "slab", [(slabs - 1, SEAM + 1), (0, SEAM)])
    keep_prev = lax.ppermute(keep, "slab", [p for p in up if p[0] != SEAM])
    keep_next = lax.ppermute(keep, "slab", [p for p in down if p[1] != SEAM])
    swap = functools.partial(lax.ppermute, axis_name="field_2", perm=[(0, 1), (1, 0)])
    sent, coef = transport_sent(noise[0], send, send_prev, send_next)
    other = swap(sent)
    kept = transport_kept(where, keep, keep_prev, keep_next, crossed, coef)
    chips = lax.axis_size(CHIPS)
    pair = (kept + other).reshape(chips, -1, NZ, NY)
    parts = lax.all_to_all(pair, CHIPS, 0, 0, tiled=True)
    average = jnp.sum(parts, 0) / F
    spread = jnp.broadcast_to(average[None], pair.shape)
    mine = lax.all_to_all(spread, CHIPS, 0, 0, tiled=True)
    updated = react(where, sent, kept, mine, swap(mine), mix_rate, evaporation, rate_matrix, stoich, prefactor)
    return updated.reshape(fields.shape)


def solution(mesh):
    split = Mesh(mesh.devices.reshape(4, 4, 2, mesh.shape["slab"]), (*FIELD, "slab"))
    return jax.shard_map(
        per_device,
        mesh=split,
        in_specs=(
            P(FIELD, None, "slab", None, None),
            P(None, "slab", None, None),
            P("slab", None, None),
            P(FIELD, None, None),
            P("slab", None, None),
            P("slab", None, None),
            P(),
            P(),
            P(),
        ),
        out_specs=P(FIELD, None, "slab", None, None),
        check_vma=False,
    )
```

```python
import functools

import jax
import jax.numpy as jnp
from jax import lax
from jax.experimental import pallas as pl
from jax.experimental.pallas import tpu as pltpu
from jax.sharding import Mesh
from jax.sharding import PartitionSpec as P

F = 32
S = 16
R = 32
SUBSTEPS = 4
X = 4
NZ = 16
NY = 128
HALF = S // 2
CHIPS = ("field_0", "field_1")
FIELD = ("field_0", "field_1", "field_2")


SLOT = {}
for _i in range(1, 3 * X - 1):
    for _k in range(SUBSTEPS):
        if _k < _i < 3 * X - 1 - _k:
            SLOT[_k, _i] = len(SLOT)
TOGETHER = 4
VMEM = pl.BlockSpec(memory_space=pltpu.VMEM)
SMEM = pl.BlockSpec(memory_space=pltpu.SMEM)
LIMIT = pltpu.CompilerParams(vmem_limit_bytes=48 * 2**20)


def pack_kernel(where_ref, fields_ref, velocity_ref, diffusivity_ref, sent_ref, kept_ref, sems):
    core = where_ref[0]
    copies = [
        pltpu.make_async_copy(fields_ref.at[0, pl.ds((1 - core) * HALF, HALF)], sent_ref.at[pl.ds(0, HALF)], sems.at[0]),
        pltpu.make_async_copy(velocity_ref, sent_ref.at[pl.ds(HALF, 3)], sems.at[1]),
        pltpu.make_async_copy(diffusivity_ref, sent_ref.at[HALF + 3], sems.at[2]),
        pltpu.make_async_copy(fields_ref.at[0, pl.ds(core * HALF, HALF)], kept_ref, sems.at[3]),
    ]
    for c in copies:
        c.start()
    for c in copies:
        c.wait()


def pack(where, fields, velocity, diffusivity):
    return pl.pallas_call(
        pack_kernel,
        out_shape=(
            jax.ShapeDtypeStruct((HALF + 4, X, NZ, NY), jnp.float32),
            jax.ShapeDtypeStruct((HALF, X, NZ, NY), jnp.float32),
        ),
        in_specs=[SMEM] + [pl.BlockSpec(memory_space=pltpu.HBM)] * 3,
        out_specs=(VMEM, VMEM),
        scratch_shapes=[pltpu.SemaphoreType.DMA((4,))],
        compiler_params=LIMIT,
        name="pack",
    )(where, *(pltpu.with_memory_space_constraint(x, pltpu.HBM) for x in (fields, velocity, diffusivity)))


def extended(where_ref, own_ref, inner_ref, outer_ref):
    odd = where_ref[1] % 2 == 1

    def layer(channel, i):
        if X <= i < 2 * X:
            return own_ref[channel, i - X]
        inner, outer = inner_ref[channel, i % X], outer_ref[channel, i % X]
        return jnp.where(odd, inner, outer) if i < X else jnp.where(odd, outer, inner)

    return layer


def coefficients(noise_ref, layer, coef_ref):
    for i in range(1, 3 * X - 1):
        diff = layer(HALF + 3, i)
        vx, vy, vz = layer(HALF, i), layer(HALF + 1, i), layer(HALF + 2, i)
        stir = jnp.sqrt(2.0 * diff)
        center = 1.0 - 6.0 * diff
        for k in range(SUBSTEPS):
            if (k, i) not in SLOT:
                continue
            hx = 0.5 * (vx - stir * noise_ref[k, 0])
            hy = 0.5 * (vy - stir * noise_ref[k, 1])
            hz = 0.5 * (vz - stir * noise_ref[k, 2])
            for n, c in enumerate((center, diff - hx, diff + hx, diff - hy, diff + hy, diff - hz, diff + hz)):
                coef_ref[SLOT[k, i], n] = c


def substeps(layer, coef_ref, out_ref):
    def some(g, carry):
        scalars = pl.ds(g * TOGETHER, TOGETHER)
        state = [layer(scalars, i) for i in range(3 * X)]
        for k in range(SUBSTEPS):
            new = [None] * (3 * X)
            for i in range(k + 1, 3 * X - 1 - k):
                c = coef_ref.at[SLOT[k, i]]
                mid = state[i]
                new[i] = (
                    (c[0][None] * mid + c[1][None] * state[i + 1] + c[2][None] * state[i - 1])
                    + (c[3][None] * pltpu.roll(mid, NY - 1, 2) + c[4][None] * pltpu.roll(mid, 1, 2))
                    + (c[5][None] * pltpu.roll(mid, NZ - 1, 1) + c[6][None] * pltpu.roll(mid, 1, 1))
                )
            state = new
        for j in range(X):
            out_ref[scalars, j] = state[X + j]
        return carry

    lax.fori_loop(0, HALF // TOGETHER, some, 0)


def sent_kernel(where_ref, noise_ref, own_ref, outer_ref, inner_ref, out_ref, coef_ref):
    layer = extended(where_ref, own_ref, inner_ref, outer_ref)
    coefficients(noise_ref, layer, coef_ref)
    substeps(layer, coef_ref, out_ref)


def transport_sent(where, noise, own, outer, inner):
    return pl.pallas_call(
        sent_kernel,
        out_shape=(
            jax.ShapeDtypeStruct((HALF, X, NZ, NY), jnp.float32),
            jax.ShapeDtypeStruct((len(SLOT), 7, NZ, NY), jnp.float32),
        ),
        in_specs=[SMEM, SMEM, VMEM, VMEM, VMEM],
        out_specs=(VMEM, VMEM),
        compiler_params=LIMIT,
        name="transport_sent",
    )(where, noise, own, outer, inner)


def kept_kernel(where_ref, own_ref, inner_ref, outer_ref, coef_ref, out_ref):
    substeps(extended(where_ref, own_ref, inner_ref, outer_ref), coef_ref, out_ref)


def transport_kept(where, own, inner, outer, coef):
    return pl.pallas_call(
        kept_kernel,
        out_shape=jax.ShapeDtypeStruct((HALF, X, NZ, NY), jnp.float32),
        in_specs=[SMEM, VMEM, VMEM, VMEM, VMEM],
        out_specs=VMEM,
        compiler_params=LIMIT,
        name="transport_kept",
    )(where, own, inner, outer, coef)


def halves(x):
    hi = x.astype(jnp.bfloat16)
    return hi, (x - hi.astype(jnp.float32)).astype(jnp.bfloat16)


def product(weights, values):
    whi, wlo = weights
    vhi, vlo = halves(values)
    return lax.dot_general(
        jnp.concatenate([whi, whi, wlo], 0),
        jnp.concatenate([vhi, vlo, vhi], 0),
        (((0,), (0,)), ((), ())),
        preferred_element_type=jnp.float32,
    )


ROWS = 16


def react_kernel(
    where_ref, sent_ref, kept_ref, mine_ref, other_ref, rate_ref, vapour_ref, rate_matrix_ref, stoich_ref, out_ref
):
    cells = X * NZ
    drive_weights = halves(rate_matrix_ref[...])
    source_weights = halves(stoich_ref[...])
    first = where_ref[0] == 0
    fuel = lax.broadcasted_iota(jnp.int32, (S, NY), 0) == 0

    def some(step, carry):
        mixed = []
        for j in range(ROWS):
            r = step * ROWS + j
            sent, kept, mine, other = (
                ref[pl.ds(r, HALF, stride=cells), :] for ref in (sent_ref, kept_ref, mine_ref, other_ref)
            )
            rate = 0.5 * rate_ref[pl.ds(r, 1), :]
            vapour = vapour_ref[pl.ds(r, 1), :]
            kept = kept - rate * (kept - mine)
            sent = sent - rate * (sent - other)
            both = jnp.concatenate([jnp.where(first, kept, sent), jnp.where(first, sent, kept)], 0)
            mixed.append(both + jnp.where(fuel, vapour, 0.0))
        mixed = jnp.concatenate(mixed, 1)
        speed = jnp.exp(2.0 * jnp.tanh(product(drive_weights, mixed)))
        updated = mixed + product(source_weights, speed)
        for j in range(ROWS):
            out_ref[pl.ds(step * ROWS + j, S, stride=cells), :] = updated[:, j * NY : (j + 1) * NY]
        return carry

    lax.fori_loop(0, cells // ROWS, some, 0, unroll=4)


def react(where, sent, kept, mine, other, rates, vapour, rate_matrix, stoich, prefactor):
    rows = X * NZ
    return pl.pallas_call(
        react_kernel,
        out_shape=jax.ShapeDtypeStruct((S * rows, NY), jnp.float32),
        in_specs=[SMEM] + [VMEM] * 8,
        out_specs=VMEM,
        compiler_params=LIMIT,
        name="react",
    )(
        where,
        *(x.reshape(HALF * rows, NY) for x in (sent, kept, mine, other)),
        rates.reshape(rows, NY),
        vapour.reshape(rows, NY),
        rate_matrix.T,
        (stoich * prefactor[None]).T,
    )


def per_device(fields, velocity, diffusivity, noise, mix_rate, evaporation, rate_matrix, stoich, prefactor):
    slabs = lax.axis_size("slab")
    where = jnp.stack([lax.axis_index("field_2"), lax.axis_index("slab")]).astype(jnp.int32)
    inner = [(i, i ^ 1) for i in range(slabs)]
    outer = [(i, i + 1 if i % 2 else i - 1) for i in range(1, slabs - 1)]
    send, keep = pack(where, fields, velocity, diffusivity)
    send_outer = lax.ppermute(send, "slab", outer)
    send_inner = lax.ppermute(send, "slab", inner)
    keep_inner = lax.ppermute(keep, "slab", inner)
    keep_outer = lax.ppermute(keep, "slab", outer)
    swap = functools.partial(lax.ppermute, axis_name="field_2", perm=[(0, 1), (1, 0)])
    sent, coef = transport_sent(where, noise[0], send, send_outer, send_inner)
    other = swap(sent)
    kept = transport_kept(where, keep, keep_inner, keep_outer, coef)
    chips = lax.axis_size(CHIPS)
    pair = (kept + other).reshape(chips, -1, NZ, NY)
    parts = lax.all_to_all(pair, CHIPS, 0, 0, tiled=True)
    average = jnp.sum(parts, 0) / F
    spread = jnp.broadcast_to(average[None], pair.shape)
    mine = lax.all_to_all(spread, CHIPS, 0, 0, tiled=True)
    updated = react(where, sent, kept, mine, swap(mine), mix_rate, evaporation, rate_matrix, stoich, prefactor)
    return updated.reshape(fields.shape)


def solution(mesh):
    split = Mesh(mesh.devices.reshape(4, 4, 2, mesh.shape["slab"]), (*FIELD, "slab"))
    return jax.shard_map(
        per_device,
        mesh=split,
        in_specs=(
            P(FIELD, None, "slab", None, None),
            P(None, "slab", None, None),
            P("slab", None, None),
            P(FIELD, None, None),
            P("slab", None, None),
            P("slab", None, None),
            P(),
            P(),
            P(),
        ),
        out_specs=P(FIELD, None, "slab", None, None),
        check_vma=False,
    )
```

```python
import functools

import jax
import jax.numpy as jnp
from jax import lax
from jax.experimental import pallas as pl
from jax.experimental.pallas import tpu as pltpu
from jax.sharding import Mesh
from jax.sharding import PartitionSpec as P

F = 32
S = 16
R = 32
SUBSTEPS = 4
X = 4
NZ = 16
NY = 128
HALF = S // 2
SEAM = 7
CHIPS = ("field_0", "field_1")
FIELD = ("field_0", "field_1", "field_2")


SLOT = {}
for _i in range(1, 3 * X - 1):
    for _k in range(SUBSTEPS):
        if _k < _i < 3 * X - 1 - _k:
            SLOT[_k, _i] = len(SLOT)
TOGETHER = 4
VMEM = pl.BlockSpec(memory_space=pltpu.VMEM)
SMEM = pl.BlockSpec(memory_space=pltpu.SMEM)
LIMIT = pltpu.CompilerParams(vmem_limit_bytes=48 * 2**20)


def at_seam(where_ref):
    return jnp.logical_or(where_ref[1] == SEAM, where_ref[1] == SEAM + 1)


def pack_kernel(where_ref, fields_ref, velocity_ref, diffusivity_ref, sent_ref, kept_ref, first_ref, sems):
    core = where_ref[0]
    sent, kept = (1 - core) * HALF, core * HALF
    first = jnp.where(at_seam(where_ref), kept, sent)
    copies = [
        pltpu.make_async_copy(source, target, sems.at[i])
        for i, (source, target) in enumerate(
            [
                (fields_ref.at[0, pl.ds(first, HALF)], first_ref.at[pl.ds(0, HALF)]),
                (velocity_ref, first_ref.at[pl.ds(HALF, 3)]),
                (diffusivity_ref, first_ref.at[HALF + 3]),
                (fields_ref.at[0, pl.ds(sent, HALF)], sent_ref.at[pl.ds(0, HALF)]),
                (velocity_ref, sent_ref.at[pl.ds(HALF, 3)]),
                (diffusivity_ref, sent_ref.at[HALF + 3]),
                (fields_ref.at[0, pl.ds(kept, HALF)], kept_ref),
            ]
        )
    ]
    for c in copies:
        c.start()
    for c in copies:
        c.wait()


def pack(where, *arrays):
    sent = jax.ShapeDtypeStruct((HALF + 4, X, NZ, NY), jnp.float32)
    return pl.pallas_call(
        pack_kernel,
        out_shape=(sent, jax.ShapeDtypeStruct((HALF, X, NZ, NY), jnp.float32), sent),
        in_specs=[SMEM] + [pl.BlockSpec(memory_space=pltpu.HBM)] * 3,
        out_specs=(VMEM, VMEM, VMEM),
        scratch_shapes=[pltpu.SemaphoreType.DMA((7,))],
        compiler_params=LIMIT,
        name="pack",
    )(where, *(pltpu.with_memory_space_constraint(x, pltpu.HBM) for x in arrays))


class Chosen:
    def __init__(self, flag, other, ref):
        self.flag, self.other, self.ref = flag, other, ref

    def __getitem__(self, at):
        other = 0.0 if self.other is None else self.other[at]
        return jnp.where(self.flag, other, self.ref[at])


def extended(where_ref, own_ref, inner_ref, outer_ref):
    odd = where_ref[1] % 2 == 1

    def layer(channel, i):
        if X <= i < 2 * X:
            return own_ref[channel, i - X]
        inner, outer = inner_ref[channel, i % X], outer_ref[channel, i % X]
        return jnp.where(odd, inner, outer) if i < X else jnp.where(odd, outer, inner)

    return layer


def coefficients(noise_ref, layer, coef_ref):
    for i in range(1, 3 * X - 1):
        diff = layer(HALF + 3, i)
        vx, vy, vz = layer(HALF, i), layer(HALF + 1, i), layer(HALF + 2, i)
        stir = jnp.sqrt(2.0 * diff)
        center = 1.0 - 6.0 * diff
        for k in range(SUBSTEPS):
            if (k, i) not in SLOT:
                continue
            hx = 0.5 * (vx - stir * noise_ref[k, 0])
            hy = 0.5 * (vy - stir * noise_ref[k, 1])
            hz = 0.5 * (vz - stir * noise_ref[k, 2])
            for n, c in enumerate((center, diff - hx, diff + hx, diff - hy, diff + hy, diff - hz, diff + hz)):
                coef_ref[SLOT[k, i], n] = c


def substeps(layer, coef_ref, out_ref):
    def some(g, carry):
        scalars = pl.ds(g * TOGETHER, TOGETHER)
        state = [layer(scalars, i) for i in range(3 * X)]
        for k in range(SUBSTEPS):
            new = [None] * (3 * X)
            for i in range(k + 1, 3 * X - 1 - k):
                c = coef_ref.at[SLOT[k, i]]
                mid = state[i]
                new[i] = (
                    (c[0][None] * mid + c[1][None] * state[i + 1] + c[2][None] * state[i - 1])
                    + (c[3][None] * pltpu.roll(mid, NY - 1, 2) + c[4][None] * pltpu.roll(mid, 1, 2))
                    + (c[5][None] * pltpu.roll(mid, NZ - 1, 1) + c[6][None] * pltpu.roll(mid, 1, 1))
                )
            state = new
        for j in range(X):
            out_ref[scalars, j] = state[X + j]
        return carry

    lax.fori_loop(0, HALF // TOGETHER, some, 0)


def sent_kernel(_, where_ref, noise_ref, own_ref, first_ref, far_ref, inner_ref, out_ref, coef_ref):
    slab = where_ref[1]
    ends = jnp.logical_or(slab == 0, slab == 2 * SEAM + 1)
    outer = Chosen(at_seam(where_ref), far_ref, Chosen(ends, None, first_ref))
    layer = extended(where_ref, own_ref, inner_ref, outer)
    coefficients(noise_ref, layer, coef_ref)
    substeps(layer, coef_ref, out_ref)


def transport_sent(*args):
    return pl.pallas_call(
        sent_kernel,
        out_shape=(
            jax.ShapeDtypeStruct((HALF, X, NZ, NY), jnp.float32),
            jax.ShapeDtypeStruct((len(SLOT), 7, NZ, NY), jnp.float32),
        ),
        in_specs=[pl.BlockSpec(memory_space=pl.ANY), SMEM, SMEM, VMEM, VMEM, VMEM, VMEM],
        out_specs=(VMEM, VMEM),
        compiler_params=LIMIT,
        name="transport_sent",
    )(*args)


def kept_kernel(where_ref, own_ref, crossed_ref, inner_ref, outer_ref, coef_ref, out_ref):
    outer = Chosen(at_seam(where_ref), crossed_ref, outer_ref)
    substeps(extended(where_ref, own_ref, inner_ref, outer), coef_ref, out_ref)


def transport_kept(*args):
    return pl.pallas_call(
        kept_kernel,
        out_shape=jax.ShapeDtypeStruct((HALF, X, NZ, NY), jnp.float32),
        in_specs=[SMEM, VMEM, VMEM, VMEM, VMEM, VMEM],
        out_specs=VMEM,
        compiler_params=LIMIT,
        name="transport_kept",
    )(*args)


def halves(x):
    hi = x.astype(jnp.bfloat16)
    return hi, (x - hi.astype(jnp.float32)).astype(jnp.bfloat16)


def product(weights, values):
    whi, wlo = weights
    vhi, vlo = halves(values)
    return lax.dot_general(
        jnp.concatenate([whi, whi, wlo], 0),
        jnp.concatenate([vhi, vlo, vhi], 0),
        (((0,), (0,)), ((), ())),
        preferred_element_type=jnp.float32,
    )


ROWS = 16


def react_kernel(
    where_ref, sent_ref, kept_ref, mine_ref, other_ref, rate_ref, vapour_ref, rate_matrix_ref, stoich_ref, out_ref
):
    cells = X * NZ
    drive_weights = halves(rate_matrix_ref[...])
    source_weights = halves(stoich_ref[...])
    first = where_ref[0] == 0
    fuel = lax.broadcasted_iota(jnp.int32, (S, NY), 0) == 0

    def some(step, carry):
        mixed = []
        for j in range(ROWS):
            r = step * ROWS + j
            sent, kept, mine, other = (
                ref[pl.ds(r, HALF, stride=cells), :] for ref in (sent_ref, kept_ref, mine_ref, other_ref)
            )
            rate = 0.5 * rate_ref[pl.ds(r, 1), :]
            vapour = vapour_ref[pl.ds(r, 1), :]
            kept = kept - rate * (kept - mine)
            sent = sent - rate * (sent - other)
            both = jnp.concatenate([jnp.where(first, kept, sent), jnp.where(first, sent, kept)], 0)
            mixed.append(both + jnp.where(fuel, vapour, 0.0))
        mixed = jnp.concatenate(mixed, 1)
        speed = jnp.exp(2.0 * jnp.tanh(product(drive_weights, mixed)))
        updated = mixed + product(source_weights, speed)
        for j in range(ROWS):
            out_ref[pl.ds(step * ROWS + j, S, stride=cells), :] = updated[:, j * NY : (j + 1) * NY]
        return carry

    lax.fori_loop(0, cells // ROWS, some, 0, unroll=4)


def react(where, sent, kept, mine, other, rates, vapour, rate_matrix, stoich, prefactor):
    rows = X * NZ
    return pl.pallas_call(
        react_kernel,
        out_shape=jax.ShapeDtypeStruct((S * rows, NY), jnp.float32),
        in_specs=[SMEM] + [VMEM] * 8,
        out_specs=VMEM,
        compiler_params=LIMIT,
        name="react",
    )(
        where,
        *(x.reshape(HALF * rows, NY) for x in (sent, kept, mine, other)),
        rates.reshape(rows, NY),
        vapour.reshape(rows, NY),
        rate_matrix.T,
        (stoich * prefactor[None]).T,
    )


def per_device(fields, velocity, diffusivity, noise, mix_rate, evaporation, rate_matrix, stoich, prefactor):
    slabs = lax.axis_size("slab")
    where = jnp.stack([lax.axis_index("field_2"), lax.axis_index("slab")]).astype(jnp.int32)
    inner = [(i, i ^ 1) for i in range(slabs)]
    outer = [(i, i + 1 if i % 2 else i - 1) for i in range(1, slabs - 1) if i not in (SEAM, SEAM + 1)]
    send, keep, first = pack(where, fields, velocity, diffusivity)
    send_outer = lax.ppermute(first, "slab", outer + [(SEAM, slabs - 1), (SEAM + 1, 0)])
    send_far = lax.ppermute(send, "slab", [(SEAM, SEAM + 1), (SEAM + 1, SEAM)])
    send_inner = lax.ppermute(send, "slab", inner)
    halfway = send_outer[:HALF]
    crossed = lax.ppermute(halfway, "slab", [(slabs - 1, SEAM + 1), (0, SEAM)])
    keep_inner = lax.ppermute(keep, "slab", inner)
    keep_outer = lax.ppermute(keep, "slab", outer)
    swap = functools.partial(lax.ppermute, axis_name="field_2", perm=[(0, 1), (1, 0)])
    sent, coef = transport_sent(halfway, where, noise[0], send, send_outer, send_far, send_inner)
    other = swap(sent)
    kept = transport_kept(where, keep, crossed, keep_inner, keep_outer, coef)
    chips = lax.axis_size(CHIPS)
    pair = (kept + other).reshape(chips, -1, NZ, NY)
    parts = lax.all_to_all(pair, CHIPS, 0, 0, tiled=True)
    average = jnp.sum(parts, 0) / F
    spread = jnp.broadcast_to(average[None], pair.shape)
    mine = lax.all_to_all(spread, CHIPS, 0, 0, tiled=True)
    updated = react(where, sent, kept, mine, swap(mine), mix_rate, evaporation, rate_matrix, stoich, prefactor)
    return updated.reshape(fields.shape)


def solution(mesh):
    split = Mesh(mesh.devices.reshape(4, 4, 2, mesh.shape["slab"]), (*FIELD, "slab"))
    return jax.shard_map(
        per_device,
        mesh=split,
        in_specs=(
            P(FIELD, None, "slab", None, None),
            P(None, "slab", None, None),
            P("slab", None, None),
            P(FIELD, None, None),
            P("slab", None, None),
            P("slab", None, None),
            P(),
            P(),
            P(),
        ),
        out_specs=P(FIELD, None, "slab", None, None),
        check_vma=False,
    )
```

```python
import functools

import jax
import jax.numpy as jnp
from jax import lax
from jax.experimental import pallas as pl
from jax.experimental.pallas import tpu as pltpu
from jax.sharding import Mesh
from jax.sharding import PartitionSpec as P

F = 32
S = 16
R = 32
SUBSTEPS = 4
X = 4
NZ = 16
NY = 128
HALF = S // 2
SEAM = 7
CHIPS = ("field_0", "field_1")
FIELD = ("field_0", "field_1", "field_2")


SLOT = {}
for _i in range(1, 3 * X - 1):
    for _k in range(SUBSTEPS):
        if _k < _i < 3 * X - 1 - _k:
            SLOT[_k, _i] = len(SLOT)
TOGETHER = 4
VMEM = pl.BlockSpec(memory_space=pltpu.VMEM)
SMEM = pl.BlockSpec(memory_space=pltpu.SMEM)
LIMIT = pltpu.CompilerParams(vmem_limit_bytes=48 * 2**20)


def at_seam(where_ref):
    return jnp.logical_or(where_ref[1] == SEAM, where_ref[1] == SEAM + 1)


def pack_kernel(where_ref, fields_ref, velocity_ref, diffusivity_ref, both_ref, sent_ref, flow_ref, kept_ref, sems):
    core = where_ref[0]
    sent = fields_ref.at[0, pl.ds((1 - core) * HALF, HALF)]
    copies = [
        pltpu.make_async_copy(source, target, sems.at[i])
        for i, (source, target) in enumerate(
            [
                (sent, sent_ref),
                (velocity_ref, flow_ref.at[pl.ds(0, 3)]),
                (diffusivity_ref, flow_ref.at[3]),
                (sent, both_ref.at[pl.ds(0, HALF)]),
                (velocity_ref, both_ref.at[pl.ds(HALF, 3)]),
                (diffusivity_ref, both_ref.at[HALF + 3]),
                (fields_ref.at[0, pl.ds(core * HALF, HALF)], kept_ref),
            ]
        )
    ]
    for c in copies:
        c.start()
    for c in copies:
        c.wait()


def pack(where, *arrays):
    channels = (HALF + 4, HALF, 4, HALF)
    return pl.pallas_call(
        pack_kernel,
        out_shape=tuple(jax.ShapeDtypeStruct((n, X, NZ, NY), jnp.float32) for n in channels),
        in_specs=[SMEM] + [pl.BlockSpec(memory_space=pltpu.HBM)] * 3,
        out_specs=(VMEM,) * 4,
        scratch_shapes=[pltpu.SemaphoreType.DMA((7,))],
        compiler_params=LIMIT,
        name="pack",
    )(where, *(pltpu.with_memory_space_constraint(x, pltpu.HBM) for x in arrays))


class Chosen:
    def __init__(self, flag, other, ref):
        self.flag, self.other, self.ref = flag, other, ref

    def __getitem__(self, at):
        other = 0.0 if self.other is None else self.other[at]
        return jnp.where(self.flag, other, self.ref[at])


def extended(where_ref, own_ref, inner_ref, outer_ref):
    odd = where_ref[1] % 2 == 1

    def layer(channel, i):
        if X <= i < 2 * X:
            return own_ref[channel, i - X]
        inner, outer = inner_ref[channel, i % X], outer_ref[channel, i % X]
        return jnp.where(odd, inner, outer) if i < X else jnp.where(odd, outer, inner)

    return layer


def coefficients(noise_ref, layer, coef_ref):
    for i in range(1, 3 * X - 1):
        diff = layer(3, i)
        vx, vy, vz = layer(0, i), layer(1, i), layer(2, i)
        stir = jnp.sqrt(2.0 * diff)
        center = 1.0 - 6.0 * diff
        for k in range(SUBSTEPS):
            if (k, i) not in SLOT:
                continue
            hx = 0.5 * (vx - stir * noise_ref[k, 0])
            hy = 0.5 * (vy - stir * noise_ref[k, 1])
            hz = 0.5 * (vz - stir * noise_ref[k, 2])
            for n, c in enumerate((center, diff - hx, diff + hx, diff - hy, diff + hy, diff - hz, diff + hz)):
                coef_ref[SLOT[k, i], n] = c


def substeps(layer, coef_ref, out_ref):
    def some(g, carry):
        scalars = pl.ds(g * TOGETHER, TOGETHER)
        state = [layer(scalars, i) for i in range(3 * X)]
        for k in range(SUBSTEPS):
            new = [None] * (3 * X)
            for i in range(k + 1, 3 * X - 1 - k):
                c = coef_ref.at[SLOT[k, i]]
                mid = state[i]
                new[i] = (
                    (c[0][None] * mid + c[1][None] * state[i + 1] + c[2][None] * state[i - 1])
                    + (c[3][None] * pltpu.roll(mid, NY - 1, 2) + c[4][None] * pltpu.roll(mid, 1, 2))
                    + (c[5][None] * pltpu.roll(mid, NZ - 1, 1) + c[6][None] * pltpu.roll(mid, 1, 1))
                )
            state = new
        for j in range(X):
            out_ref[scalars, j] = state[X + j]
        return carry

    lax.fori_loop(0, HALF // TOGETHER, some, 0)


def sent_kernel(where_ref, noise_ref, own_ref, first_ref, flow_ref, inner_ref, crossed_ref, out_ref, coef_ref):
    slab = where_ref[1]
    ends = jnp.logical_or(slab == 0, slab == 2 * SEAM + 1)
    outer = Chosen(at_seam(where_ref), crossed_ref, Chosen(ends, None, first_ref))
    flow = pl.ds(HALF, 4)
    coefficients(noise_ref, extended(where_ref, own_ref.at[flow], inner_ref.at[flow], flow_ref), coef_ref)
    substeps(extended(where_ref, own_ref, inner_ref, outer), coef_ref, out_ref)


def transport_sent(*args):
    return pl.pallas_call(
        sent_kernel,
        out_shape=(
            jax.ShapeDtypeStruct((HALF, X, NZ, NY), jnp.float32),
            jax.ShapeDtypeStruct((len(SLOT), 7, NZ, NY), jnp.float32),
        ),
        in_specs=[SMEM, SMEM] + [VMEM] * 5,
        out_specs=(VMEM, VMEM),
        compiler_params=LIMIT,
        name="transport_sent",
    )(*args)


def kept_kernel(where_ref, coef_ref, own_ref, inner_ref, outer_ref, out_ref):
    substeps(extended(where_ref, own_ref, inner_ref, outer_ref), coef_ref, out_ref)


def transport_kept(*args):
    return pl.pallas_call(
        kept_kernel,
        out_shape=jax.ShapeDtypeStruct((HALF, X, NZ, NY), jnp.float32),
        in_specs=[SMEM] + [VMEM] * 4,
        out_specs=VMEM,
        compiler_params=LIMIT,
        name="transport_kept",
    )(*args)


def halves(x):
    hi = x.astype(jnp.bfloat16)
    return hi, (x - hi.astype(jnp.float32)).astype(jnp.bfloat16)


def product(weights, values):
    whi, wlo = weights
    vhi, vlo = halves(values)
    return lax.dot_general(
        jnp.concatenate([whi, whi, wlo], 0),
        jnp.concatenate([vhi, vlo, vhi], 0),
        (((0,), (0,)), ((), ())),
        preferred_element_type=jnp.float32,
    )


ROWS = 16


def react_kernel(
    where_ref, sent_ref, kept_ref, mine_ref, other_ref, rate_ref, vapour_ref, rate_matrix_ref, stoich_ref, out_ref
):
    cells = X * NZ
    drive_weights = halves(rate_matrix_ref[...])
    source_weights = halves(stoich_ref[...])
    first = where_ref[0] == 0
    fuel = lax.broadcasted_iota(jnp.int32, (S, NY), 0) == 0

    def some(step, carry):
        mixed = []
        for j in range(ROWS):
            r = step * ROWS + j
            sent, kept, mine, other = (
                ref[pl.ds(r, HALF, stride=cells), :] for ref in (sent_ref, kept_ref, mine_ref, other_ref)
            )
            rate = 0.5 * rate_ref[pl.ds(r, 1), :]
            vapour = vapour_ref[pl.ds(r, 1), :]
            kept = kept - rate * (kept - mine)
            sent = sent - rate * (sent - other)
            both = jnp.concatenate([jnp.where(first, kept, sent), jnp.where(first, sent, kept)], 0)
            mixed.append(both + jnp.where(fuel, vapour, 0.0))
        mixed = jnp.concatenate(mixed, 1)
        speed = jnp.exp(2.0 * jnp.tanh(product(drive_weights, mixed)))
        updated = mixed + product(source_weights, speed)
        for j in range(ROWS):
            out_ref[pl.ds(step * ROWS + j, S, stride=cells), :] = updated[:, j * NY : (j + 1) * NY]
        return carry

    lax.fori_loop(0, cells // ROWS, some, 0, unroll=4)


def react(where, sent, kept, mine, other, rates, vapour, rate_matrix, stoich, prefactor):
    rows = X * NZ
    return pl.pallas_call(
        react_kernel,
        out_shape=jax.ShapeDtypeStruct((S * rows, NY), jnp.float32),
        in_specs=[SMEM] + [VMEM] * 8,
        out_specs=VMEM,
        compiler_params=LIMIT,
        name="react",
    )(
        where,
        *(x.reshape(HALF * rows, NY) for x in (sent, kept, mine, other)),
        rates.reshape(rows, NY),
        vapour.reshape(rows, NY),
        rate_matrix.T,
        (stoich * prefactor[None]).T,
    )


def per_device(fields, velocity, diffusivity, noise, mix_rate, evaporation, rate_matrix, stoich, prefactor):
    slabs = lax.axis_size("slab")
    where = jnp.stack([lax.axis_index("field_2"), lax.axis_index("slab")]).astype(jnp.int32)
    inner = [(i, i ^ 1) for i in range(slabs)]
    outer = [(i, i + 1 if i % 2 else i - 1) for i in range(1, slabs - 1)]
    near = [p for p in outer if p[0] not in (SEAM, SEAM + 1)]
    both, send, flow, keep = pack(where, fields, velocity, diffusivity)
    send_outer = lax.ppermute(send, "slab", near + [(SEAM, 0), (SEAM + 1, slabs - 1)])
    flow_outer = lax.ppermute(flow, "slab", outer)
    both_inner = lax.ppermute(both, "slab", inner)
    crossed = lax.ppermute(send_outer, "slab", [(0, SEAM + 1), (slabs - 1, SEAM)])
    keep_inner = lax.ppermute(keep, "slab", inner)
    after, _ = lax.optimization_barrier((keep, send_outer))
    keep_outer = lax.ppermute(after, "slab", outer)
    swap = functools.partial(lax.ppermute, axis_name="field_2", perm=[(0, 1), (1, 0)])
    sent, coef = transport_sent(where, noise[0], both, send_outer, flow_outer, both_inner, crossed)
    other = swap(sent)
    kept = transport_kept(where, coef, keep, keep_inner, keep_outer)
    chips = lax.axis_size(CHIPS)
    pair = (kept + other).reshape(chips, -1, NZ, NY)
    parts = lax.all_to_all(pair, CHIPS, 0, 0, tiled=True)
    average = jnp.sum(parts, 0) / F
    spread = jnp.broadcast_to(average[None], pair.shape)
    mine = lax.all_to_all(spread, CHIPS, 0, 0, tiled=True)
    updated = react(where, sent, kept, mine, swap(mine), mix_rate, evaporation, rate_matrix, stoich, prefactor)
    return updated.reshape(fields.shape)


def solution(mesh):
    split = Mesh(mesh.devices.reshape(4, 4, 2, mesh.shape["slab"]), (*FIELD, "slab"))
    return jax.shard_map(
        per_device,
        mesh=split,
        in_specs=(
            P(FIELD, None, "slab", None, None),
            P(None, "slab", None, None),
            P("slab", None, None),
            P(FIELD, None, None),
            P("slab", None, None),
            P("slab", None, None),
            P(),
            P(),
            P(),
        ),
        out_specs=P(FIELD, None, "slab", None, None),
        check_vma=False,
    )
```

```python
import functools

import jax
import jax.numpy as jnp
from jax import lax
from jax.experimental import pallas as pl
from jax.experimental.pallas import tpu as pltpu
from jax.sharding import Mesh
from jax.sharding import PartitionSpec as P

F = 32
S = 16
R = 32
SUBSTEPS = 4
X = 4
NZ = 16
NY = 128
HALF = S // 2
SEAM = 7
CHIPS = ("field_0", "field_1")
FIELD = ("field_0", "field_1", "field_2")


SLOT = {}
for _i in range(1, 3 * X - 1):
    for _k in range(SUBSTEPS):
        if _k < _i < 3 * X - 1 - _k:
            SLOT[_k, _i] = len(SLOT)
TOGETHER = 4
VMEM = pl.BlockSpec(memory_space=pltpu.VMEM)
SMEM = pl.BlockSpec(memory_space=pltpu.SMEM)
LIMIT = pltpu.CompilerParams(vmem_limit_bytes=48 * 2**20)


def at_seam(where_ref):
    return jnp.logical_or(where_ref[1] == SEAM, where_ref[1] == SEAM + 1)


def pack_kernel(where_ref, fields_ref, velocity_ref, diffusivity_ref, sent_ref, kept_ref, sems):
    core = where_ref[0]
    copies = [
        pltpu.make_async_copy(source, target, sems.at[i])
        for i, (source, target) in enumerate(
            [
                (fields_ref.at[0, pl.ds((1 - core) * HALF, HALF)], sent_ref.at[pl.ds(0, HALF)]),
                (velocity_ref, sent_ref.at[pl.ds(HALF, 3)]),
                (diffusivity_ref, sent_ref.at[HALF + 3]),
                (fields_ref.at[0, pl.ds(core * HALF, HALF)], kept_ref),
            ]
        )
    ]
    for c in copies:
        c.start()
    for c in copies:
        c.wait()


def pack(where, *arrays):
    return pl.pallas_call(
        pack_kernel,
        out_shape=tuple(jax.ShapeDtypeStruct((n, X, NZ, NY), jnp.float32) for n in (HALF + 4, HALF)),
        in_specs=[SMEM] + [pl.BlockSpec(memory_space=pltpu.HBM)] * 3,
        out_specs=(VMEM, VMEM),
        scratch_shapes=[pltpu.SemaphoreType.DMA((4,))],
        compiler_params=LIMIT,
        name="pack",
    )(where, *(pltpu.with_memory_space_constraint(x, pltpu.HBM) for x in arrays))


class Chosen:
    def __init__(self, flag, other, ref):
        self.flag, self.other, self.ref = flag, other, ref

    def __getitem__(self, at):
        other = 0.0 if self.other is None else self.other[at]
        return jnp.where(self.flag, other, self.ref[at])


def extended(where_ref, own_ref, inner_ref, outer_ref):
    odd = where_ref[1] % 2 == 1

    def layer(channel, i):
        if X <= i < 2 * X:
            return own_ref[channel, i - X]
        inner, outer = inner_ref[channel, i % X], outer_ref[channel, i % X]
        return jnp.where(odd, inner, outer) if i < X else jnp.where(odd, outer, inner)

    return layer


def coefficients(noise_ref, layer, coef_ref):
    for i in range(1, 3 * X - 1):
        diff = layer(HALF + 3, i)
        vx, vy, vz = layer(HALF, i), layer(HALF + 1, i), layer(HALF + 2, i)
        stir = jnp.sqrt(2.0 * diff)
        center = 1.0 - 6.0 * diff
        for k in range(SUBSTEPS):
            if (k, i) not in SLOT:
                continue
            hx = 0.5 * (vx - stir * noise_ref[k, 0])
            hy = 0.5 * (vy - stir * noise_ref[k, 1])
            hz = 0.5 * (vz - stir * noise_ref[k, 2])
            for n, c in enumerate((center, diff - hx, diff + hx, diff - hy, diff + hy, diff - hz, diff + hz)):
                coef_ref[SLOT[k, i], n] = c


def substeps(layer, coef_ref, out_ref):
    def some(g, carry):
        scalars = pl.ds(g * TOGETHER, TOGETHER)
        state = [layer(scalars, i) for i in range(3 * X)]
        for k in range(SUBSTEPS):
            new = [None] * (3 * X)
            for i in range(k + 1, 3 * X - 1 - k):
                c = coef_ref.at[SLOT[k, i]]
                mid = state[i]
                new[i] = (
                    (c[0][None] * mid + c[1][None] * state[i + 1] + c[2][None] * state[i - 1])
                    + (c[3][None] * pltpu.roll(mid, NY - 1, 2) + c[4][None] * pltpu.roll(mid, 1, 2))
                    + (c[5][None] * pltpu.roll(mid, NZ - 1, 1) + c[6][None] * pltpu.roll(mid, 1, 1))
                )
            state = new
        for j in range(X):
            out_ref[scalars, j] = state[X + j]
        return carry

    lax.fori_loop(0, HALF // TOGETHER, some, 0)


def sent_kernel(where_ref, noise_ref, own_ref, first_ref, inner_ref, crossed_ref, out_ref, coef_ref):
    slab = where_ref[1]
    ends = jnp.logical_or(slab == 0, slab == 2 * SEAM + 1)
    outer = Chosen(at_seam(where_ref), crossed_ref, Chosen(ends, None, first_ref))
    layer = extended(where_ref, own_ref, inner_ref, outer)
    coefficients(noise_ref, layer, coef_ref)
    substeps(layer, coef_ref, out_ref)


def transport_sent(*args):
    return pl.pallas_call(
        sent_kernel,
        out_shape=(
            jax.ShapeDtypeStruct((HALF, X, NZ, NY), jnp.float32),
            jax.ShapeDtypeStruct((len(SLOT), 7, NZ, NY), jnp.float32),
        ),
        in_specs=[SMEM, SMEM] + [VMEM] * 4,
        out_specs=(VMEM, VMEM),
        compiler_params=LIMIT,
        name="transport_sent",
    )(*args)


def kept_kernel(where_ref, coef_ref, own_ref, outer_ref, inner_ref, out_ref):
    substeps(extended(where_ref, own_ref, inner_ref, outer_ref), coef_ref, out_ref)


def transport_kept(*args):
    return pl.pallas_call(
        kept_kernel,
        out_shape=jax.ShapeDtypeStruct((HALF, X, NZ, NY), jnp.float32),
        in_specs=[SMEM] + [VMEM] * 4,
        out_specs=VMEM,
        compiler_params=LIMIT,
        name="transport_kept",
    )(*args)


def halves(x):
    hi = x.astype(jnp.bfloat16)
    return hi, (x - hi.astype(jnp.float32)).astype(jnp.bfloat16)


def product(weights, values):
    whi, wlo = weights
    vhi, vlo = halves(values)
    return lax.dot_general(
        jnp.concatenate([whi, whi, wlo], 0),
        jnp.concatenate([vhi, vlo, vhi], 0),
        (((0,), (0,)), ((), ())),
        preferred_element_type=jnp.float32,
    )


ROWS = 16


def react_kernel(
    where_ref, sent_ref, kept_ref, mine_ref, other_ref, rate_ref, vapour_ref, rate_matrix_ref, stoich_ref, out_ref
):
    cells = X * NZ
    drive_weights = halves(rate_matrix_ref[...])
    source_weights = halves(stoich_ref[...])
    first = where_ref[0] == 0
    fuel = lax.broadcasted_iota(jnp.int32, (S, NY), 0) == 0

    def some(step, carry):
        mixed = []
        for j in range(ROWS):
            r = step * ROWS + j
            sent, kept, mine, other = (
                ref[pl.ds(r, HALF, stride=cells), :] for ref in (sent_ref, kept_ref, mine_ref, other_ref)
            )
            rate = 0.5 * rate_ref[pl.ds(r, 1), :]
            vapour = vapour_ref[pl.ds(r, 1), :]
            kept = kept - rate * (kept - mine)
            sent = sent - rate * (sent - other)
            both = jnp.concatenate([jnp.where(first, kept, sent), jnp.where(first, sent, kept)], 0)
            mixed.append(both + jnp.where(fuel, vapour, 0.0))
        mixed = jnp.concatenate(mixed, 1)
        speed = jnp.exp(2.0 * jnp.tanh(product(drive_weights, mixed)))
        updated = mixed + product(source_weights, speed)
        for j in range(ROWS):
            out_ref[pl.ds(step * ROWS + j, S, stride=cells), :] = updated[:, j * NY : (j + 1) * NY]
        return carry

    lax.fori_loop(0, cells // ROWS, some, 0, unroll=4)


def react(where, sent, kept, mine, other, rates, vapour, rate_matrix, stoich, prefactor):
    rows = X * NZ
    return pl.pallas_call(
        react_kernel,
        out_shape=jax.ShapeDtypeStruct((S * rows, NY), jnp.float32),
        in_specs=[SMEM] + [VMEM] * 8,
        out_specs=VMEM,
        compiler_params=LIMIT,
        name="react",
    )(
        where,
        *(x.reshape(HALF * rows, NY) for x in (sent, kept, mine, other)),
        rates.reshape(rows, NY),
        vapour.reshape(rows, NY),
        rate_matrix.T,
        (stoich * prefactor[None]).T,
    )


def per_device(fields, velocity, diffusivity, noise, mix_rate, evaporation, rate_matrix, stoich, prefactor):
    slabs = lax.axis_size("slab")
    where = jnp.stack([lax.axis_index("field_2"), lax.axis_index("slab")]).astype(jnp.int32)
    inner = [(i, i ^ 1) for i in range(slabs)]
    outer = [(i, i + 1 if i % 2 else i - 1) for i in range(1, slabs - 1)]
    near = [p for p in outer if p[0] not in (SEAM, SEAM + 1)]
    send, keep = pack(where, fields, velocity, diffusivity)
    send_outer = lax.ppermute(send, "slab", near + [(SEAM, 0), (SEAM + 1, slabs - 1)])
    send_inner = lax.ppermute(send, "slab", inner)
    crossed = lax.ppermute(send_outer, "slab", [(0, SEAM + 1), (slabs - 1, SEAM)])
    after, _ = lax.optimization_barrier((keep, send_outer))
    keep_outer = lax.ppermute(after, "slab", outer)
    keep_inner = lax.ppermute(keep, "slab", inner)
    swap = functools.partial(lax.ppermute, axis_name="field_2", perm=[(0, 1), (1, 0)])
    sent, coef = transport_sent(where, noise[0], send, send_outer, send_inner, crossed)
    other = swap(sent)
    kept = transport_kept(where, coef, keep, keep_outer, keep_inner)
    chips = lax.axis_size(CHIPS)
    pair = (kept + other).reshape(chips, -1, NZ, NY)
    parts = lax.all_to_all(pair, CHIPS, 0, 0, tiled=True)
    average = jnp.sum(parts, 0) / F
    spread = jnp.broadcast_to(average[None], pair.shape)
    mine = lax.all_to_all(spread, CHIPS, 0, 0, tiled=True)
    updated = react(where, sent, kept, mine, swap(mine), mix_rate, evaporation, rate_matrix, stoich, prefactor)
    return updated.reshape(fields.shape)


def solution(mesh):
    split = Mesh(mesh.devices.reshape(4, 4, 2, mesh.shape["slab"]), (*FIELD, "slab"))
    return jax.shard_map(
        per_device,
        mesh=split,
        in_specs=(
            P(FIELD, None, "slab", None, None),
            P(None, "slab", None, None),
            P("slab", None, None),
            P(FIELD, None, None),
            P("slab", None, None),
            P("slab", None, None),
            P(),
            P(),
            P(),
        ),
        out_specs=P(FIELD, None, "slab", None, None),
        check_vma=False,
    )
```

```python
import functools

import jax
import jax.numpy as jnp
from jax import lax
from jax.experimental import pallas as pl
from jax.experimental.pallas import tpu as pltpu
from jax.sharding import Mesh
from jax.sharding import PartitionSpec as P

F = 32
S = 16
R = 32
SUBSTEPS = 4
X = 4
NZ = 16
NY = 128
HALF = S // 2
CHIPS = ("field_0", "field_1")
FIELD = ("field_0", "field_1", "field_2")
ALIKE = ("field_0", "field_2")


SLOT = {}
for _i in range(1, 3 * X - 1):
    for _k in range(SUBSTEPS):
        if _k < _i < 3 * X - 1 - _k:
            SLOT[_k, _i] = len(SLOT)
TOGETHER = 4
VMEM = pl.BlockSpec(memory_space=pltpu.VMEM)
SMEM = pl.BlockSpec(memory_space=pltpu.SMEM)
LIMIT = pltpu.CompilerParams(vmem_limit_bytes=48 * 2**20)


def pack_kernel(where_ref, fields_ref, velocity_ref, diffusivity_ref, part_ref, sent_ref, kept_ref, sems):
    core, part = where_ref[0], where_ref[2]
    layers = pl.ds(part % 2 * 2, 2)
    copies = [
        pltpu.make_async_copy(fields_ref.at[0, pl.ds((1 - core) * HALF, HALF)], sent_ref, sems.at[1]),
        pltpu.make_async_copy(fields_ref.at[0, pl.ds(core * HALF, HALF)], kept_ref, sems.at[2]),
    ]
    for c in copies:
        c.start()

    @pl.when(part < 6)
    def _():
        copy = pltpu.make_async_copy(velocity_ref.at[part // 2, layers], part_ref, sems.at[0])
        copy.start()
        copy.wait()

    @pl.when(part >= 6)
    def _():
        copy = pltpu.make_async_copy(diffusivity_ref.at[layers], part_ref, sems.at[0])
        copy.start()
        copy.wait()

    for c in copies:
        c.wait()


def pack(where, *arrays):
    half = jax.ShapeDtypeStruct((HALF, X, NZ, NY), jnp.float32)
    return pl.pallas_call(
        pack_kernel,
        out_shape=(jax.ShapeDtypeStruct((2, NZ, NY), jnp.float32), half, half),
        in_specs=[SMEM] + [pl.BlockSpec(memory_space=pltpu.HBM)] * 3,
        out_specs=(VMEM, VMEM, VMEM),
        scratch_shapes=[pltpu.SemaphoreType.DMA((3,))],
        compiler_params=LIMIT,
        name="pack",
    )(where, *(pltpu.with_memory_space_constraint(x, pltpu.HBM) for x in arrays))


def extended(where_ref, own_ref, inner_ref, outer_ref):
    odd = where_ref[1] % 2 == 1

    def layer(channel, i):
        if X <= i < 2 * X:
            return own_ref[channel, i - X]
        inner, outer = inner_ref[channel, i % X], outer_ref[channel, i % X]
        return jnp.where(odd, inner, outer) if i < X else jnp.where(odd, outer, inner)

    return layer


def coefficients_kernel(where_ref, noise_ref, parts_ref, velocity_ref, diffusivity_ref, coef_ref):
    odd = where_ref[1] % 2 == 1

    def layer(channel, i):
        if X <= i < 2 * X:
            return velocity_ref[channel, i - X] if channel < 3 else diffusivity_ref[i - X]
        j = i % X
        outer, inner = (parts_ref[2 * channel + j // 2, n, j % 2] for n in range(2))
        return jnp.where(odd, inner, outer) if i < X else jnp.where(odd, outer, inner)

    for i in range(1, 3 * X - 1):
        vx, vy, vz, diff = (layer(n, i) for n in range(4))
        stir = jnp.sqrt(2.0 * diff)
        center = 1.0 - 6.0 * diff
        for k in range(SUBSTEPS):
            if (k, i) not in SLOT:
                continue
            hx = 0.5 * (vx - stir * noise_ref[k, 0])
            hy = 0.5 * (vy - stir * noise_ref[k, 1])
            hz = 0.5 * (vz - stir * noise_ref[k, 2])
            for n, c in enumerate((center, diff - hx, diff + hx, diff - hy, diff + hy, diff - hz, diff + hz)):
                coef_ref[SLOT[k, i], n] = c


def coefficients(*args):
    return pl.pallas_call(
        coefficients_kernel,
        out_shape=jax.ShapeDtypeStruct((len(SLOT), 7, NZ, NY), jnp.float32),
        in_specs=[SMEM, SMEM, VMEM, VMEM, VMEM],
        out_specs=VMEM,
        compiler_params=LIMIT,
        name="coefficients",
    )(*args)


def substeps(layer, coef_ref, out_ref):
    def some(g, carry):
        scalars = pl.ds(g * TOGETHER, TOGETHER)
        state = [layer(scalars, i) for i in range(3 * X)]
        for k in range(SUBSTEPS):
            new = [None] * (3 * X)
            for i in range(k + 1, 3 * X - 1 - k):
                c = coef_ref.at[SLOT[k, i]]
                mid = state[i]
                new[i] = (
                    (c[0][None] * mid + c[1][None] * state[i + 1] + c[2][None] * state[i - 1])
                    + (c[3][None] * pltpu.roll(mid, NY - 1, 2) + c[4][None] * pltpu.roll(mid, 1, 2))
                    + (c[5][None] * pltpu.roll(mid, NZ - 1, 1) + c[6][None] * pltpu.roll(mid, 1, 1))
                )
            state = new
        for j in range(X):
            out_ref[scalars, j] = state[X + j]
        return carry

    lax.fori_loop(0, HALF // TOGETHER, some, 0)


def transport_kernel(where_ref, coef_ref, own_ref, outer_ref, inner_ref, out_ref):
    substeps(extended(where_ref, own_ref, inner_ref, outer_ref), coef_ref, out_ref)


def transport(name, *args):
    return pl.pallas_call(
        transport_kernel,
        out_shape=jax.ShapeDtypeStruct((HALF, X, NZ, NY), jnp.float32),
        in_specs=[SMEM] + [VMEM] * 4,
        out_specs=VMEM,
        compiler_params=LIMIT,
        name=name,
    )(*args)


def halves(x):
    hi = x.astype(jnp.bfloat16)
    return hi, (x - hi.astype(jnp.float32)).astype(jnp.bfloat16)


def product(weights, values):
    whi, wlo = weights
    vhi, vlo = halves(values)
    return lax.dot_general(
        jnp.concatenate([whi, whi, wlo], 0),
        jnp.concatenate([vhi, vlo, vhi], 0),
        (((0,), (0,)), ((), ())),
        preferred_element_type=jnp.float32,
    )


ROWS = 16


def react_kernel(
    where_ref, sent_ref, kept_ref, mine_ref, other_ref, rate_ref, vapour_ref, rate_matrix_ref, stoich_ref, out_ref
):
    cells = X * NZ
    drive_weights = halves(rate_matrix_ref[...])
    source_weights = halves(stoich_ref[...])
    first = where_ref[0] == 0
    fuel = lax.broadcasted_iota(jnp.int32, (S, NY), 0) == 0

    def some(step, carry):
        mixed = []
        for j in range(ROWS):
            r = step * ROWS + j
            sent, kept, mine, other = (
                ref[pl.ds(r, HALF, stride=cells), :] for ref in (sent_ref, kept_ref, mine_ref, other_ref)
            )
            rate = 0.5 * rate_ref[pl.ds(r, 1), :]
            vapour = vapour_ref[pl.ds(r, 1), :]
            kept = kept - rate * (kept - mine)
            sent = sent - rate * (sent - other)
            both = jnp.concatenate([jnp.where(first, kept, sent), jnp.where(first, sent, kept)], 0)
            mixed.append(both + jnp.where(fuel, vapour, 0.0))
        mixed = jnp.concatenate(mixed, 1)
        speed = jnp.exp(2.0 * jnp.tanh(product(drive_weights, mixed)))
        updated = mixed + product(source_weights, speed)
        for j in range(ROWS):
            out_ref[pl.ds(step * ROWS + j, S, stride=cells), :] = updated[:, j * NY : (j + 1) * NY]
        return carry

    lax.fori_loop(0, cells // ROWS, some, 0, unroll=4)


def react(where, sent, kept, mine, other, rates, vapour, rate_matrix, stoich, prefactor):
    rows = X * NZ
    return pl.pallas_call(
        react_kernel,
        out_shape=jax.ShapeDtypeStruct((S * rows, NY), jnp.float32),
        in_specs=[SMEM] + [VMEM] * 8,
        out_specs=VMEM,
        compiler_params=LIMIT,
        name="react",
    )(
        where,
        *(x.reshape(HALF * rows, NY) for x in (sent, kept, mine, other)),
        rates.reshape(rows, NY),
        vapour.reshape(rows, NY),
        rate_matrix.T,
        (stoich * prefactor[None]).T,
    )


def per_device(fields, velocity, diffusivity, noise, mix_rate, evaporation, rate_matrix, stoich, prefactor):
    slabs = lax.axis_size("slab")
    where = jnp.stack([lax.axis_index("field_2"), lax.axis_index("slab"), lax.axis_index(ALIKE)]).astype(jnp.int32)
    inner = [(i, i ^ 1) for i in range(slabs)]
    outer = [(i, i + 1 if i % 2 else i - 1) for i in range(1, slabs - 1)]
    part, send, keep = pack(where, fields, velocity, diffusivity)
    part_outer = lax.ppermute(part, "slab", outer)
    part_inner = lax.ppermute(part, "slab", inner)
    send_outer = lax.ppermute(send, "slab", outer)
    send_inner = lax.ppermute(send, "slab", inner)
    keep_outer = lax.ppermute(keep, "slab", outer)
    keep_inner = lax.ppermute(keep, "slab", inner)
    parts = jnp.stack([part_outer, part_inner])
    parts = lax.all_to_all(jnp.broadcast_to(parts, (lax.axis_size(ALIKE), *parts.shape)), ALIKE, 0, 0, tiled=True)
    coef = coefficients(where, noise[0], parts, velocity, diffusivity)
    swap = functools.partial(lax.ppermute, axis_name="field_2", perm=[(0, 1), (1, 0)])
    sent = transport("transport_sent", where, coef, send, send_outer, send_inner)
    other = swap(sent)
    kept = transport("transport_kept", where, coef, keep, keep_outer, keep_inner)
    chips = lax.axis_size(CHIPS)
    pair = (kept + other).reshape(chips, -1, NZ, NY)
    parts = lax.all_to_all(pair, CHIPS, 0, 0, tiled=True)
    average = jnp.sum(parts, 0) / F
    spread = jnp.broadcast_to(average[None], pair.shape)
    mine = lax.all_to_all(spread, CHIPS, 0, 0, tiled=True)
    updated = react(where, sent, kept, mine, swap(mine), mix_rate, evaporation, rate_matrix, stoich, prefactor)
    return updated.reshape(fields.shape)


def solution(mesh):
    split = Mesh(mesh.devices.reshape(4, 4, 2, mesh.shape["slab"]), (*FIELD, "slab"))
    return jax.shard_map(
        per_device,
        mesh=split,
        in_specs=(
            P(FIELD, None, "slab", None, None),
            P(None, "slab", None, None),
            P("slab", None, None),
            P(FIELD, None, None),
            P("slab", None, None),
            P("slab", None, None),
            P(),
            P(),
            P(),
        ),
        out_specs=P(FIELD, None, "slab", None, None),
        check_vma=False,
    )
```

```python
import functools

import jax
import jax.numpy as jnp
from jax import lax
from jax.experimental import pallas as pl
from jax.experimental.pallas import tpu as pltpu
from jax.sharding import Mesh
from jax.sharding import PartitionSpec as P

F = 32
S = 16
R = 32
SUBSTEPS = 4
X = 4
NZ = 16
NY = 128
HALF = S // 2
CHIPS = ("field_0", "field_1")
FIELD = ("field_0", "field_1", "field_2")


SLOT = {}
for _i in range(1, 3 * X - 1):
    for _k in range(SUBSTEPS):
        if _k < _i < 3 * X - 1 - _k:
            SLOT[_k, _i] = len(SLOT)
TOGETHER = 4
VMEM = pl.BlockSpec(memory_space=pltpu.VMEM)
SMEM = pl.BlockSpec(memory_space=pltpu.SMEM)
LIMIT = pltpu.CompilerParams(vmem_limit_bytes=48 * 2**20)


USED = X - 1
CELLS = X * HALF


def pack_kernel(where_ref, fields_ref, velocity_ref, diffusivity_ref, outer_ref, inner_ref, kept_ref, sems):
    core, odd = where_ref[0], where_ref[1] % 2
    copies = []

    def copy(source, target):
        copies.append(pltpu.make_async_copy(source, target, sems.at[len(copies)]))
        copies[-1].start()

    for target, first, head in (
        (outer_ref, (1 - core) * HALF, odd),
        (inner_ref, (1 - core) * HALF, 1 - odd),
        (kept_ref, core * HALF, None),
    ):
        for j in range(X):
            copy(fields_ref.at[0, pl.ds(first, HALF), j], target.at[pl.ds(j * HALF, HALF)])
        if head is None:
            continue
        for n in range(4):
            source = velocity_ref.at[n] if n < 3 else diffusivity_ref
            copy(source.at[pl.ds(head, USED)], target.at[pl.ds(CELLS + n * USED, USED)])
    for c in copies:
        c.wait()


def pack(where, *arrays):
    planes = (CELLS + 4 * USED, CELLS + 4 * USED, CELLS)
    return pl.pallas_call(
        pack_kernel,
        out_shape=tuple(jax.ShapeDtypeStruct((n, NZ, NY), jnp.float32) for n in planes),
        in_specs=[SMEM] + [pl.BlockSpec(memory_space=pltpu.HBM)] * 3,
        out_specs=(VMEM,) * 3,
        scratch_shapes=[pltpu.SemaphoreType.DMA((3 * X + 8,))],
        compiler_params=LIMIT,
        name="pack",
    )(where, *(pltpu.with_memory_space_constraint(x, pltpu.HBM) for x in arrays))


def extended(where_ref, own_ref, inner_ref, outer_ref):
    odd = where_ref[1] % 2 == 1

    def layer(some, i):
        at = pl.ds(i % X * HALF + some * TOGETHER, TOGETHER)
        if X <= i < 2 * X:
            return own_ref[at]
        inner, outer = inner_ref[at], outer_ref[at]
        return jnp.where(odd, inner, outer) if i < X else jnp.where(odd, outer, inner)

    return layer


def flow(where_ref, own_inner_ref, own_outer_ref, inner_ref, outer_ref):
    odd = where_ref[1] % 2 == 1

    def layer(channel, i):
        def pick(if_odd, if_even, j):
            at = CELLS + channel * USED + j
            return jnp.where(odd, if_odd[at], if_even[at])

        if i < X:
            return pick(inner_ref, outer_ref, i - 1)
        if i >= 2 * X:
            return pick(outer_ref, inner_ref, i - 2 * X)
        if i == X:
            return pick(own_inner_ref, own_outer_ref, 0)
        return pick(own_outer_ref, own_inner_ref, i - X - 1)

    return layer


def coefficients(noise_ref, layer, coef_ref):
    for i in range(1, 3 * X - 1):
        vx, vy, vz, diff = (layer(n, i) for n in range(4))
        stir = jnp.sqrt(2.0 * diff)
        center = 1.0 - 6.0 * diff
        for k in range(SUBSTEPS):
            if (k, i) not in SLOT:
                continue
            hx = 0.5 * (vx - stir * noise_ref[k, 0])
            hy = 0.5 * (vy - stir * noise_ref[k, 1])
            hz = 0.5 * (vz - stir * noise_ref[k, 2])
            for n, c in enumerate((center, diff - hx, diff + hx, diff - hy, diff + hy, diff - hz, diff + hz)):
                coef_ref[SLOT[k, i], n] = c


def substeps(layer, coef_ref, out_ref):
    def some(g, carry):
        scalars = pl.ds(g * TOGETHER, TOGETHER)
        state = [layer(g, i) for i in range(3 * X)]
        for k in range(SUBSTEPS):
            new = [None] * (3 * X)
            for i in range(k + 1, 3 * X - 1 - k):
                c = coef_ref.at[SLOT[k, i]]
                mid = state[i]
                new[i] = (
                    (c[0][None] * mid + c[1][None] * state[i + 1] + c[2][None] * state[i - 1])
                    + (c[3][None] * pltpu.roll(mid, NY - 1, 2) + c[4][None] * pltpu.roll(mid, 1, 2))
                    + (c[5][None] * pltpu.roll(mid, NZ - 1, 1) + c[6][None] * pltpu.roll(mid, 1, 1))
                )
            state = new
        for j in range(X):
            out_ref[scalars, j] = state[X + j]
        return carry

    lax.fori_loop(0, HALF // TOGETHER, some, 0)


def sent_kernel(where_ref, noise_ref, own_outer_ref, own_inner_ref, outer_ref, inner_ref, out_ref, coef_ref):
    coefficients(noise_ref, flow(where_ref, own_inner_ref, own_outer_ref, inner_ref, outer_ref), coef_ref)
    substeps(extended(where_ref, own_outer_ref, inner_ref, outer_ref), coef_ref, out_ref)


def transport_sent(*args):
    return pl.pallas_call(
        sent_kernel,
        out_shape=(
            jax.ShapeDtypeStruct((HALF, X, NZ, NY), jnp.float32),
            jax.ShapeDtypeStruct((len(SLOT), 7, NZ, NY), jnp.float32),
        ),
        in_specs=[SMEM, SMEM] + [VMEM] * 4,
        out_specs=(VMEM, VMEM),
        compiler_params=LIMIT,
        name="transport_sent",
    )(*args)


def kept_kernel(where_ref, own_ref, inner_ref, outer_ref, coef_ref, out_ref):
    substeps(extended(where_ref, own_ref, inner_ref, outer_ref), coef_ref, out_ref)


def transport_kept(where, own, inner, outer, coef):
    return pl.pallas_call(
        kept_kernel,
        out_shape=jax.ShapeDtypeStruct((HALF, X, NZ, NY), jnp.float32),
        in_specs=[SMEM, VMEM, VMEM, VMEM, VMEM],
        out_specs=VMEM,
        compiler_params=LIMIT,
        name="transport_kept",
    )(where, own, inner, outer, coef)


def halves(x):
    hi = x.astype(jnp.bfloat16)
    return hi, (x - hi.astype(jnp.float32)).astype(jnp.bfloat16)


def product(weights, values):
    whi, wlo = weights
    vhi, vlo = halves(values)
    return lax.dot_general(
        jnp.concatenate([whi, whi, wlo], 0),
        jnp.concatenate([vhi, vlo, vhi], 0),
        (((0,), (0,)), ((), ())),
        preferred_element_type=jnp.float32,
    )


ROWS = 16


def react_kernel(
    where_ref, sent_ref, kept_ref, mine_ref, other_ref, rate_ref, vapour_ref, rate_matrix_ref, stoich_ref, out_ref
):
    cells = X * NZ
    drive_weights = halves(rate_matrix_ref[...])
    source_weights = halves(stoich_ref[...])
    first = where_ref[0] == 0
    fuel = lax.broadcasted_iota(jnp.int32, (S, NY), 0) == 0

    def some(step, carry):
        mixed = []
        for j in range(ROWS):
            r = step * ROWS + j
            sent, kept, mine, other = (
                ref[pl.ds(r, HALF, stride=cells), :] for ref in (sent_ref, kept_ref, mine_ref, other_ref)
            )
            rate = 0.5 * rate_ref[pl.ds(r, 1), :]
            vapour = vapour_ref[pl.ds(r, 1), :]
            kept = kept - rate * (kept - mine)
            sent = sent - rate * (sent - other)
            both = jnp.concatenate([jnp.where(first, kept, sent), jnp.where(first, sent, kept)], 0)
            mixed.append(both + jnp.where(fuel, vapour, 0.0))
        mixed = jnp.concatenate(mixed, 1)
        speed = jnp.exp(2.0 * jnp.tanh(product(drive_weights, mixed)))
        updated = mixed + product(source_weights, speed)
        for j in range(ROWS):
            out_ref[pl.ds(step * ROWS + j, S, stride=cells), :] = updated[:, j * NY : (j + 1) * NY]
        return carry

    lax.fori_loop(0, cells // ROWS, some, 0, unroll=4)


def react(where, sent, kept, mine, other, rates, vapour, rate_matrix, stoich, prefactor):
    rows = X * NZ
    return pl.pallas_call(
        react_kernel,
        out_shape=jax.ShapeDtypeStruct((S * rows, NY), jnp.float32),
        in_specs=[SMEM] + [VMEM] * 8,
        out_specs=VMEM,
        compiler_params=LIMIT,
        name="react",
    )(
        where,
        *(x.reshape(HALF * rows, NY) for x in (sent, kept, mine, other)),
        rates.reshape(rows, NY),
        vapour.reshape(rows, NY),
        rate_matrix.T,
        (stoich * prefactor[None]).T,
    )


def per_device(fields, velocity, diffusivity, noise, mix_rate, evaporation, rate_matrix, stoich, prefactor):
    slabs = lax.axis_size("slab")
    where = jnp.stack([lax.axis_index("field_2"), lax.axis_index("slab")]).astype(jnp.int32)
    inner = [(i, i ^ 1) for i in range(slabs)]
    outer = [(i, i + 1 if i % 2 else i - 1) for i in range(1, slabs - 1)]
    to_outer, to_inner, keep = pack(where, fields, velocity, diffusivity)
    from_outer = lax.ppermute(to_outer, "slab", outer)
    from_inner = lax.ppermute(to_inner, "slab", inner)
    keep_inner = lax.ppermute(keep, "slab", inner)
    keep_outer = lax.ppermute(keep, "slab", outer)
    swap = functools.partial(lax.ppermute, axis_name="field_2", perm=[(0, 1), (1, 0)])
    sent, coef = transport_sent(where, noise[0], to_outer, to_inner, from_outer, from_inner)
    other = swap(sent)
    kept = transport_kept(where, keep, keep_inner, keep_outer, coef)
    chips = lax.axis_size(CHIPS)
    pair = (kept + other).reshape(chips, -1, NZ, NY)
    parts = lax.all_to_all(pair, CHIPS, 0, 0, tiled=True)
    average = jnp.sum(parts, 0) / F
    spread = jnp.broadcast_to(average[None], pair.shape)
    mine = lax.all_to_all(spread, CHIPS, 0, 0, tiled=True)
    updated = react(where, sent, kept, mine, swap(mine), mix_rate, evaporation, rate_matrix, stoich, prefactor)
    return updated.reshape(fields.shape)


def solution(mesh):
    split = Mesh(mesh.devices.reshape(4, 4, 2, mesh.shape["slab"]), (*FIELD, "slab"))
    return jax.shard_map(
        per_device,
        mesh=split,
        in_specs=(
            P(FIELD, None, "slab", None, None),
            P(None, "slab", None, None),
            P("slab", None, None),
            P(FIELD, None, None),
            P("slab", None, None),
            P("slab", None, None),
            P(),
            P(),
            P(),
        ),
        out_specs=P(FIELD, None, "slab", None, None),
        check_vma=False,
    )
```

```python
import functools

import jax
import jax.numpy as jnp
from jax import lax
from jax.experimental import pallas as pl
from jax.experimental.pallas import tpu as pltpu
from jax.sharding import Mesh
from jax.sharding import PartitionSpec as P

F = 32
S = 16
R = 32
SUBSTEPS = 4
X = 4
NZ = 16
NY = 128
HALF = S // 2
CHIPS = ("field_0", "field_1")
FIELD = ("field_0", "field_1", "field_2")


SLOT = {}
for _i in range(1, 3 * X - 1):
    for _k in range(SUBSTEPS):
        if _k < _i < 3 * X - 1 - _k:
            SLOT[_k, _i] = len(SLOT)
TOGETHER = 8
VMEM = pl.BlockSpec(memory_space=pltpu.VMEM)
SMEM = pl.BlockSpec(memory_space=pltpu.SMEM)
LIMIT = pltpu.CompilerParams(vmem_limit_bytes=48 * 2**20)


USED = X - 1
CELLS = X * HALF


def pack_kernel(where_ref, fields_ref, velocity_ref, diffusivity_ref, outer_ref, inner_ref, kept_ref, sems):
    core, odd = where_ref[0], where_ref[1] % 2
    copies = []

    def copy(source, target):
        copies.append(pltpu.make_async_copy(source, target, sems.at[len(copies)]))
        copies[-1].start()

    for target, first, head in (
        (outer_ref, (1 - core) * HALF, odd),
        (inner_ref, (1 - core) * HALF, 1 - odd),
        (kept_ref, core * HALF, None),
    ):
        for j in range(X):
            copy(fields_ref.at[0, pl.ds(first, HALF), j], target.at[pl.ds(j * HALF, HALF)])
        if head is None:
            continue
        for n in range(4):
            source = velocity_ref.at[n] if n < 3 else diffusivity_ref
            copy(source.at[pl.ds(head, USED)], target.at[pl.ds(CELLS + n * USED, USED)])
    for c in copies:
        c.wait()


def pack(where, *arrays):
    planes = (CELLS + 4 * USED, CELLS + 4 * USED, CELLS)
    return pl.pallas_call(
        pack_kernel,
        out_shape=tuple(jax.ShapeDtypeStruct((n, NZ, NY), jnp.float32) for n in planes),
        in_specs=[SMEM] + [pl.BlockSpec(memory_space=pltpu.HBM)] * 3,
        out_specs=(VMEM,) * 3,
        scratch_shapes=[pltpu.SemaphoreType.DMA((3 * X + 8,))],
        compiler_params=LIMIT,
        name="pack",
    )(where, *(pltpu.with_memory_space_constraint(x, pltpu.HBM) for x in arrays))


def extended(where_ref, own_ref, inner_ref, outer_ref):
    odd = where_ref[1] % 2 == 1

    def layer(some, i):
        at = pl.ds(i % X * HALF + some * TOGETHER, TOGETHER)
        if X <= i < 2 * X:
            return own_ref[at]
        inner, outer = inner_ref[at], outer_ref[at]
        return jnp.where(odd, inner, outer) if i < X else jnp.where(odd, outer, inner)

    return layer


def flow(where_ref, own_inner_ref, own_outer_ref, inner_ref, outer_ref):
    odd = where_ref[1] % 2 == 1

    def layer(channel, i):
        def pick(if_odd, if_even, j):
            at = CELLS + channel * USED + j
            return jnp.where(odd, if_odd[at], if_even[at])

        if i < X:
            return pick(inner_ref, outer_ref, i - 1)
        if i >= 2 * X:
            return pick(outer_ref, inner_ref, i - 2 * X)
        if i == X:
            return pick(own_inner_ref, own_outer_ref, 0)
        return pick(own_outer_ref, own_inner_ref, i - X - 1)

    return layer


def coefficients(noise_ref, layer, coef_ref):
    for i in range(1, 3 * X - 1):
        vx, vy, vz, diff = (layer(n, i) for n in range(4))
        stir = jnp.sqrt(2.0 * diff)
        center = 1.0 - 6.0 * diff
        for k in range(SUBSTEPS):
            if (k, i) not in SLOT:
                continue
            hx = 0.5 * (vx - stir * noise_ref[k, 0])
            hy = 0.5 * (vy - stir * noise_ref[k, 1])
            hz = 0.5 * (vz - stir * noise_ref[k, 2])
            for n, c in enumerate((center, diff - hx, diff + hx, diff - hy, diff + hy, diff - hz, diff + hz)):
                coef_ref[SLOT[k, i], n] = c


def substeps(layer, coef_ref, out_ref):
    def some(g, carry):
        scalars = pl.ds(g * TOGETHER, TOGETHER)
        state = [layer(g, i) for i in range(3 * X)]
        for k in range(SUBSTEPS):
            new = [None] * (3 * X)
            for i in range(k + 1, 3 * X - 1 - k):
                c = coef_ref.at[SLOT[k, i]]
                mid = state[i]
                new[i] = (
                    (c[0][None] * mid + c[1][None] * state[i + 1] + c[2][None] * state[i - 1])
                    + (c[3][None] * pltpu.roll(mid, NY - 1, 2) + c[4][None] * pltpu.roll(mid, 1, 2))
                    + (c[5][None] * pltpu.roll(mid, NZ - 1, 1) + c[6][None] * pltpu.roll(mid, 1, 1))
                )
            state = new
        for j in range(X):
            out_ref[scalars, j] = state[X + j]
        return carry

    lax.fori_loop(0, HALF // TOGETHER, some, 0)


def sent_kernel(where_ref, noise_ref, own_outer_ref, own_inner_ref, outer_ref, inner_ref, out_ref, coef_ref):
    coefficients(noise_ref, flow(where_ref, own_inner_ref, own_outer_ref, inner_ref, outer_ref), coef_ref)
    substeps(extended(where_ref, own_outer_ref, inner_ref, outer_ref), coef_ref, out_ref)


def transport_sent(*args):
    return pl.pallas_call(
        sent_kernel,
        out_shape=(
            jax.ShapeDtypeStruct((HALF, X, NZ, NY), jnp.float32),
            jax.ShapeDtypeStruct((len(SLOT), 7, NZ, NY), jnp.float32),
        ),
        in_specs=[SMEM, SMEM] + [VMEM] * 4,
        out_specs=(VMEM, VMEM),
        compiler_params=LIMIT,
        name="transport_sent",
    )(*args)


def kept_kernel(where_ref, own_ref, inner_ref, outer_ref, coef_ref, out_ref):
    substeps(extended(where_ref, own_ref, inner_ref, outer_ref), coef_ref, out_ref)


def transport_kept(where, own, inner, outer, coef):
    return pl.pallas_call(
        kept_kernel,
        out_shape=jax.ShapeDtypeStruct((HALF, X, NZ, NY), jnp.float32),
        in_specs=[SMEM, VMEM, VMEM, VMEM, VMEM],
        out_specs=VMEM,
        compiler_params=LIMIT,
        name="transport_kept",
    )(where, own, inner, outer, coef)


def halves(x):
    hi = x.astype(jnp.bfloat16)
    return hi, (x - hi.astype(jnp.float32)).astype(jnp.bfloat16)


def product(weights, values):
    whi, wlo = weights
    vhi, vlo = halves(values)
    return lax.dot_general(
        jnp.concatenate([whi, whi, wlo], 0),
        jnp.concatenate([vhi, vlo, vhi], 0),
        (((0,), (0,)), ((), ())),
        preferred_element_type=jnp.float32,
    )


ROWS = 32


def react_kernel(
    where_ref,
    sent_ref,
    kept_ref,
    mine_ref,
    other_ref,
    rate_ref,
    vapour_ref,
    rate_matrix_ref,
    stoich_ref,
    out_ref,
    done_ref,
    sems,
):
    cells = X * NZ
    drive_weights = halves(rate_matrix_ref[...])
    source_weights = halves(stoich_ref[...])
    first = where_ref[0] == 0
    fuel = lax.broadcasted_iota(jnp.int32, (S, NY), 0) == 0
    copies = []
    for block in range(cells // ROWS):
        mixed = []
        for r in range(block * ROWS, (block + 1) * ROWS):
            sent, kept, mine, other = (
                ref[pl.ds(r, HALF, stride=cells), :] for ref in (sent_ref, kept_ref, mine_ref, other_ref)
            )
            rate = 0.5 * rate_ref[pl.ds(r, 1), :]
            vapour = vapour_ref[pl.ds(r, 1), :]
            kept = kept - rate * (kept - mine)
            sent = sent - rate * (sent - other)
            both = jnp.concatenate([jnp.where(first, kept, sent), jnp.where(first, sent, kept)], 0)
            mixed.append(both + jnp.where(fuel, vapour, 0.0))
        mixed = jnp.concatenate(mixed, 1)
        speed = jnp.exp(2.0 * jnp.tanh(product(drive_weights, mixed)))
        updated = mixed + product(source_weights, speed)
        for j in range(ROWS):
            done_ref.at[block][pl.ds(j, S, stride=ROWS), :] = updated[:, j * NY : (j + 1) * NY]
        for s in range(S):
            copies.append(
                pltpu.make_async_copy(
                    done_ref.at[block, pl.ds(s * ROWS, ROWS)],
                    out_ref.at[pl.ds(s * cells + block * ROWS, ROWS)],
                    sems.at[len(copies)],
                )
            )
            copies[-1].start()
    for c in copies:
        c.wait()


def react(where, sent, kept, mine, other, rates, vapour, rate_matrix, stoich, prefactor):
    rows = X * NZ
    return pl.pallas_call(
        react_kernel,
        out_shape=jax.ShapeDtypeStruct((S * rows, NY), jnp.float32),
        in_specs=[SMEM] + [VMEM] * 8,
        out_specs=pl.BlockSpec(memory_space=pltpu.HBM),
        scratch_shapes=[
            pltpu.VMEM((rows // ROWS, S * ROWS, NY), jnp.float32),
            pltpu.SemaphoreType.DMA((S * rows // ROWS,)),
        ],
        compiler_params=LIMIT,
        name="react",
    )(
        where,
        *(x.reshape(HALF * rows, NY) for x in (sent, kept, mine, other)),
        rates.reshape(rows, NY),
        vapour.reshape(rows, NY),
        rate_matrix.T,
        (stoich * prefactor[None]).T,
    )


def per_device(fields, velocity, diffusivity, noise, mix_rate, evaporation, rate_matrix, stoich, prefactor):
    slabs = lax.axis_size("slab")
    where = jnp.stack([lax.axis_index("field_2"), lax.axis_index("slab")]).astype(jnp.int32)
    inner = [(i, i ^ 1) for i in range(slabs)]
    outer = [(i, i + 1 if i % 2 else i - 1) for i in range(1, slabs - 1)]
    to_outer, to_inner, keep = pack(where, fields, velocity, diffusivity)
    from_outer = lax.ppermute(to_outer, "slab", outer)
    from_inner = lax.ppermute(to_inner, "slab", inner)
    keep_inner = lax.ppermute(keep, "slab", inner)
    keep_outer = lax.ppermute(keep, "slab", outer)
    swap = functools.partial(lax.ppermute, axis_name="field_2", perm=[(0, 1), (1, 0)])
    sent, coef = transport_sent(where, noise[0], to_outer, to_inner, from_outer, from_inner)
    other = swap(sent)
    kept = transport_kept(where, keep, keep_inner, keep_outer, coef)
    chips = lax.axis_size(CHIPS)
    pair = (kept + other).reshape(chips, -1, NZ, NY)
    parts = lax.all_to_all(pair, CHIPS, 0, 0, tiled=True)
    average = jnp.sum(parts, 0) / F
    spread = jnp.broadcast_to(average[None], pair.shape)
    mine = lax.all_to_all(spread, CHIPS, 0, 0, tiled=True)
    updated = react(where, sent, kept, mine, swap(mine), mix_rate, evaporation, rate_matrix, stoich, prefactor)
    return updated.reshape(fields.shape)


def solution(mesh):
    split = Mesh(mesh.devices.reshape(4, 4, 2, mesh.shape["slab"]), (*FIELD, "slab"))
    return jax.shard_map(
        per_device,
        mesh=split,
        in_specs=(
            P(FIELD, None, "slab", None, None),
            P(None, "slab", None, None),
            P("slab", None, None),
            P(FIELD, None, None),
            P("slab", None, None),
            P("slab", None, None),
            P(),
            P(),
            P(),
        ),
        out_specs=P(FIELD, None, "slab", None, None),
        check_vma=False,
    )
```

```python
import functools

import jax
import jax.numpy as jnp
from jax import lax
from jax.experimental import pallas as pl
from jax.experimental.pallas import tpu as pltpu
from jax.sharding import Mesh
from jax.sharding import PartitionSpec as P

F = 32
S = 16
R = 32
SUBSTEPS = 4
X = 4
NZ = 16
NY = 128
HALF = S // 2
CHIPS = ("field_1", "field_0")
FIELD = ("field_0", "field_1", "field_2")


SLOT = {}
for _i in range(1, 3 * X - 1):
    for _k in range(SUBSTEPS):
        if _k < _i < 3 * X - 1 - _k:
            SLOT[_k, _i] = len(SLOT)
TOGETHER = 8
VMEM = pl.BlockSpec(memory_space=pltpu.VMEM)
SMEM = pl.BlockSpec(memory_space=pltpu.SMEM)
LIMIT = pltpu.CompilerParams(vmem_limit_bytes=48 * 2**20)


USED = X - 1
CELLS = X * HALF


def pack_kernel(where_ref, fields_ref, velocity_ref, diffusivity_ref, outer_ref, inner_ref, kept_ref, sems):
    core, odd = where_ref[0], where_ref[1] % 2
    copies = []

    def copy(source, target):
        copies.append(pltpu.make_async_copy(source, target, sems.at[len(copies)]))
        copies[-1].start()

    for target, first, head in (
        (outer_ref, (1 - core) * HALF, odd),
        (inner_ref, (1 - core) * HALF, 1 - odd),
        (kept_ref, core * HALF, None),
    ):
        for j in range(X):
            copy(fields_ref.at[0, pl.ds(first, HALF), j], target.at[pl.ds(j * HALF, HALF)])
        if head is None:
            continue
        for n in range(4):
            source = velocity_ref.at[n] if n < 3 else diffusivity_ref
            copy(source.at[pl.ds(head, USED)], target.at[pl.ds(CELLS + n * USED, USED)])
    for c in copies:
        c.wait()


def pack(where, *arrays):
    planes = (CELLS + 4 * USED, CELLS + 4 * USED, CELLS)
    return pl.pallas_call(
        pack_kernel,
        out_shape=tuple(jax.ShapeDtypeStruct((n, NZ, NY), jnp.float32) for n in planes),
        in_specs=[SMEM] + [pl.BlockSpec(memory_space=pltpu.HBM)] * 3,
        out_specs=(VMEM,) * 3,
        scratch_shapes=[pltpu.SemaphoreType.DMA((3 * X + 8,))],
        compiler_params=LIMIT,
        name="pack",
    )(where, *(pltpu.with_memory_space_constraint(x, pltpu.HBM) for x in arrays))


def extended(where_ref, own_ref, inner_ref, outer_ref):
    odd = where_ref[1] % 2 == 1

    def layer(some, i):
        at = pl.ds(i % X * HALF + some * TOGETHER, TOGETHER)
        if X <= i < 2 * X:
            return own_ref[at]
        inner, outer = inner_ref[at], outer_ref[at]
        return jnp.where(odd, inner, outer) if i < X else jnp.where(odd, outer, inner)

    return layer


def flow(where_ref, own_inner_ref, own_outer_ref, inner_ref, outer_ref):
    odd = where_ref[1] % 2 == 1

    def layer(channel, i):
        def pick(if_odd, if_even, j):
            at = CELLS + channel * USED + j
            return jnp.where(odd, if_odd[at], if_even[at])

        if i < X:
            return pick(inner_ref, outer_ref, i - 1)
        if i >= 2 * X:
            return pick(outer_ref, inner_ref, i - 2 * X)
        if i == X:
            return pick(own_inner_ref, own_outer_ref, 0)
        return pick(own_outer_ref, own_inner_ref, i - X - 1)

    return layer


def coefficients(noise_ref, layer, coef_ref):
    for i in range(1, 3 * X - 1):
        vx, vy, vz, diff = (layer(n, i) for n in range(4))
        stir = jnp.sqrt(2.0 * diff)
        center = 1.0 - 6.0 * diff
        for k in range(SUBSTEPS):
            if (k, i) not in SLOT:
                continue
            hx = 0.5 * (vx - stir * noise_ref[k, 0])
            hy = 0.5 * (vy - stir * noise_ref[k, 1])
            hz = 0.5 * (vz - stir * noise_ref[k, 2])
            for n, c in enumerate((center, diff - hx, diff + hx, diff - hy, diff + hy, diff - hz, diff + hz)):
                coef_ref[SLOT[k, i], n] = c


def substeps(layer, coef_ref, out_ref):
    def some(g, carry):
        scalars = pl.ds(g * TOGETHER, TOGETHER)
        state = [layer(g, i) for i in range(3 * X)]
        for k in range(SUBSTEPS):
            new = [None] * (3 * X)
            for i in range(k + 1, 3 * X - 1 - k):
                c = coef_ref.at[SLOT[k, i]]
                mid = state[i]
                new[i] = (
                    (c[0][None] * mid + c[1][None] * state[i + 1] + c[2][None] * state[i - 1])
                    + (c[3][None] * pltpu.roll(mid, NY - 1, 2) + c[4][None] * pltpu.roll(mid, 1, 2))
                    + (c[5][None] * pltpu.roll(mid, NZ - 1, 1) + c[6][None] * pltpu.roll(mid, 1, 1))
                )
            state = new
        for j in range(X):
            out_ref[scalars, j] = state[X + j]
        return carry

    lax.fori_loop(0, HALF // TOGETHER, some, 0)


def sent_kernel(where_ref, noise_ref, own_outer_ref, own_inner_ref, outer_ref, inner_ref, out_ref, coef_ref):
    coefficients(noise_ref, flow(where_ref, own_inner_ref, own_outer_ref, inner_ref, outer_ref), coef_ref)
    substeps(extended(where_ref, own_outer_ref, inner_ref, outer_ref), coef_ref, out_ref)


def transport_sent(*args):
    return pl.pallas_call(
        sent_kernel,
        out_shape=(
            jax.ShapeDtypeStruct((HALF, X, NZ, NY), jnp.float32),
            jax.ShapeDtypeStruct((len(SLOT), 7, NZ, NY), jnp.float32),
        ),
        in_specs=[SMEM, SMEM] + [VMEM] * 4,
        out_specs=(VMEM, VMEM),
        compiler_params=LIMIT,
        name="transport_sent",
    )(*args)


def kept_kernel(where_ref, own_ref, outer_ref, inner_ref, coef_ref, out_ref):
    substeps(extended(where_ref, own_ref, inner_ref, outer_ref), coef_ref, out_ref)


def transport_kept(where, own, outer, inner, coef):
    return pl.pallas_call(
        kept_kernel,
        out_shape=jax.ShapeDtypeStruct((HALF, X, NZ, NY), jnp.float32),
        in_specs=[SMEM, VMEM, VMEM, VMEM, VMEM],
        out_specs=VMEM,
        compiler_params=LIMIT,
        name="transport_kept",
    )(where, own, outer, inner, coef)


def halves(x):
    hi = x.astype(jnp.bfloat16)
    return hi, (x - hi.astype(jnp.float32)).astype(jnp.bfloat16)


def product(weights, values):
    whi, wlo = weights
    vhi, vlo = halves(values)
    return lax.dot_general(
        jnp.concatenate([whi, whi, wlo], 0),
        jnp.concatenate([vhi, vlo, vhi], 0),
        (((0,), (0,)), ((), ())),
        preferred_element_type=jnp.float32,
    )


ROWS = 32


def react_kernel(
    where_ref,
    sent_ref,
    kept_ref,
    mine_ref,
    other_ref,
    rate_ref,
    vapour_ref,
    rate_matrix_ref,
    stoich_ref,
    out_ref,
    done_ref,
    sems,
):
    cells = X * NZ
    drive_weights = halves(rate_matrix_ref[...])
    source_weights = halves(stoich_ref[...])
    first = where_ref[0] == 0
    fuel = lax.broadcasted_iota(jnp.int32, (S, NY), 0) == 0
    copies = []
    for block in range(cells // ROWS):
        mixed = []
        for r in range(block * ROWS, (block + 1) * ROWS):
            sent, kept, mine, other = (
                ref[pl.ds(r, HALF, stride=cells), :] for ref in (sent_ref, kept_ref, mine_ref, other_ref)
            )
            rate = 0.5 * rate_ref[pl.ds(r, 1), :]
            vapour = vapour_ref[pl.ds(r, 1), :]
            kept = kept - rate * (kept - mine)
            sent = sent - rate * (sent - other)
            both = jnp.concatenate([jnp.where(first, kept, sent), jnp.where(first, sent, kept)], 0)
            mixed.append(both + jnp.where(fuel, vapour, 0.0))
        mixed = jnp.concatenate(mixed, 1)
        speed = jnp.exp(2.0 * jnp.tanh(product(drive_weights, mixed)))
        updated = mixed + product(source_weights, speed)
        for j in range(ROWS):
            done_ref.at[block][pl.ds(j, S, stride=ROWS), :] = updated[:, j * NY : (j + 1) * NY]
        for s in range(S):
            copies.append(
                pltpu.make_async_copy(
                    done_ref.at[block, pl.ds(s * ROWS, ROWS)],
                    out_ref.at[pl.ds(s * cells + block * ROWS, ROWS)],
                    sems.at[len(copies)],
                )
            )
            copies[-1].start()
    for c in copies:
        c.wait()


def react(where, sent, kept, mine, other, rates, vapour, rate_matrix, stoich, prefactor):
    rows = X * NZ
    return pl.pallas_call(
        react_kernel,
        out_shape=jax.ShapeDtypeStruct((S * rows, NY), jnp.float32),
        in_specs=[SMEM] + [VMEM] * 8,
        out_specs=pl.BlockSpec(memory_space=pltpu.HBM),
        scratch_shapes=[
            pltpu.VMEM((rows // ROWS, S * ROWS, NY), jnp.float32),
            pltpu.SemaphoreType.DMA((S * rows // ROWS,)),
        ],
        compiler_params=LIMIT,
        name="react",
    )(
        where,
        *(x.reshape(HALF * rows, NY) for x in (sent, kept, mine, other)),
        rates.reshape(rows, NY),
        vapour.reshape(rows, NY),
        rate_matrix.T,
        (stoich * prefactor[None]).T,
    )


def per_device(fields, velocity, diffusivity, noise, mix_rate, evaporation, rate_matrix, stoich, prefactor):
    slabs = lax.axis_size("slab")
    where = jnp.stack([lax.axis_index("field_2"), lax.axis_index("slab")]).astype(jnp.int32)
    inner = [(i, i ^ 1) for i in range(slabs)]
    outer = [(i, i + 1 if i % 2 else i - 1) for i in range(1, slabs - 1)]
    to_outer, to_inner, keep = pack(where, fields, velocity, diffusivity)
    from_outer = lax.ppermute(to_outer, "slab", outer)
    from_inner = lax.ppermute(to_inner, "slab", inner)
    keep_outer = lax.ppermute(keep, "slab", outer)
    keep_inner = lax.ppermute(keep, "slab", inner)
    swap = functools.partial(lax.ppermute, axis_name="field_2", perm=[(0, 1), (1, 0)])
    sent, coef = transport_sent(where, noise[0], to_outer, to_inner, from_outer, from_inner)
    other = swap(sent)
    kept = transport_kept(where, keep, keep_outer, keep_inner, coef)
    chips = lax.axis_size(CHIPS)
    pair = (kept + other).reshape(chips, -1, NZ, NY)
    parts = lax.all_to_all(pair, CHIPS, 0, 0, tiled=True)
    average = jnp.sum(parts, 0) / F
    spread = jnp.broadcast_to(average[None], pair.shape)
    mine = lax.all_to_all(spread, CHIPS, 0, 0, tiled=True)
    updated = react(where, sent, kept, mine, swap(mine), mix_rate, evaporation, rate_matrix, stoich, prefactor)
    return updated.reshape(fields.shape)


def solution(mesh):
    split = Mesh(mesh.devices.reshape(4, 4, 2, mesh.shape["slab"]), (*FIELD, "slab"))
    return jax.shard_map(
        per_device,
        mesh=split,
        in_specs=(
            P(FIELD, None, "slab", None, None),
            P(None, "slab", None, None),
            P("slab", None, None),
            P(FIELD, None, None),
            P("slab", None, None),
            P("slab", None, None),
            P(),
            P(),
            P(),
        ),
        out_specs=P(FIELD, None, "slab", None, None),
        check_vma=False,
    )
```

```python
import functools

import jax
import jax.numpy as jnp
from jax import lax
from jax.experimental import pallas as pl
from jax.experimental.pallas import tpu as pltpu
from jax.sharding import Mesh
from jax.sharding import PartitionSpec as P

F = 32
S = 16
R = 32
SUBSTEPS = 4
X = 4
NZ = 16
NY = 128
HALF = S // 2
CHIPS = ("field_0", "field_1")
FIELD = ("field_0", "field_1", "field_2")


SLOT = {}
for _i in range(1, 3 * X - 1):
    for _k in range(SUBSTEPS):
        if _k < _i < 3 * X - 1 - _k:
            SLOT[_k, _i] = len(SLOT)
TOGETHER = 8
VMEM = pl.BlockSpec(memory_space=pltpu.VMEM)
SMEM = pl.BlockSpec(memory_space=pltpu.SMEM)
LIMIT = pltpu.CompilerParams(vmem_limit_bytes=48 * 2**20)


USED = X - 1
CELLS = X * HALF


def pack_kernel(where_ref, fields_ref, velocity_ref, diffusivity_ref, outer_ref, inner_ref, kept_ref, sems):
    core, odd = where_ref[0], where_ref[1] % 2
    copies = []

    def copy(source, target):
        copies.append(pltpu.make_async_copy(source, target, sems.at[len(copies)]))
        copies[-1].start()

    for target, first, head in (
        (outer_ref, (1 - core) * HALF, odd),
        (inner_ref, (1 - core) * HALF, 1 - odd),
        (kept_ref, core * HALF, None),
    ):
        for j in range(X):
            copy(fields_ref.at[0, pl.ds(first, HALF), j], target.at[pl.ds(j * HALF, HALF)])
        if head is None:
            continue
        for n in range(4):
            source = velocity_ref.at[n] if n < 3 else diffusivity_ref
            copy(source.at[pl.ds(head, USED)], target.at[pl.ds(CELLS + n * USED, USED)])
    for c in copies:
        c.wait()


def pack(where, *arrays):
    planes = (CELLS + 4 * USED, CELLS + 4 * USED, CELLS)
    return pl.pallas_call(
        pack_kernel,
        out_shape=tuple(jax.ShapeDtypeStruct((n, NZ, NY), jnp.float32) for n in planes),
        in_specs=[SMEM] + [pl.BlockSpec(memory_space=pltpu.HBM)] * 3,
        out_specs=(VMEM,) * 3,
        scratch_shapes=[pltpu.SemaphoreType.DMA((3 * X + 8,))],
        compiler_params=LIMIT,
        name="pack",
    )(where, *(pltpu.with_memory_space_constraint(x, pltpu.HBM) for x in arrays))


def extended(where_ref, own_ref, inner_ref, outer_ref):
    odd = where_ref[1] % 2 == 1

    def layer(some, i):
        at = pl.ds(i % X * HALF + some * TOGETHER, TOGETHER)
        if X <= i < 2 * X:
            return own_ref[at]
        inner, outer = inner_ref[at], outer_ref[at]
        return jnp.where(odd, inner, outer) if i < X else jnp.where(odd, outer, inner)

    return layer


def flow(where_ref, own_inner_ref, own_outer_ref, inner_ref, outer_ref):
    odd = where_ref[1] % 2 == 1

    def layer(channel, i):
        def pick(if_odd, if_even, j):
            at = CELLS + channel * USED + j
            return jnp.where(odd, if_odd[at], if_even[at])

        if i < X:
            return pick(inner_ref, outer_ref, i - 1)
        if i >= 2 * X:
            return pick(outer_ref, inner_ref, i - 2 * X)
        if i == X:
            return pick(own_inner_ref, own_outer_ref, 0)
        return pick(own_outer_ref, own_inner_ref, i - X - 1)

    return layer


def coefficients(noise_ref, layer, coef_ref):
    for i in range(1, 3 * X - 1):
        vx, vy, vz, diff = (layer(n, i) for n in range(4))
        stir = jnp.sqrt(2.0 * diff)
        center = 1.0 - 6.0 * diff
        for k in range(SUBSTEPS):
            if (k, i) not in SLOT:
                continue
            hx = 0.5 * (vx - stir * noise_ref[k, 0])
            hy = 0.5 * (vy - stir * noise_ref[k, 1])
            hz = 0.5 * (vz - stir * noise_ref[k, 2])
            for n, c in enumerate((center, diff - hx, diff + hx, diff - hy, diff + hy, diff - hz, diff + hz)):
                coef_ref[SLOT[k, i], n] = c


def substeps(layer, coef_ref, out_ref):
    def some(g, carry):
        scalars = pl.ds(g * TOGETHER, TOGETHER)
        state = [layer(g, i) for i in range(3 * X)]
        for k in range(SUBSTEPS):
            new = [None] * (3 * X)
            for i in range(k + 1, 3 * X - 1 - k):
                c = coef_ref.at[SLOT[k, i]]
                mid = state[i]
                new[i] = (
                    (c[0][None] * mid + c[1][None] * state[i + 1] + c[2][None] * state[i - 1])
                    + (c[3][None] * pltpu.roll(mid, NY - 1, 2) + c[4][None] * pltpu.roll(mid, 1, 2))
                    + (c[5][None] * pltpu.roll(mid, NZ - 1, 1) + c[6][None] * pltpu.roll(mid, 1, 1))
                )
            state = new
        for j in range(X):
            out_ref[scalars, j] = state[X + j]
        return carry

    lax.fori_loop(0, HALF // TOGETHER, some, 0)


def sent_kernel(where_ref, noise_ref, own_outer_ref, own_inner_ref, outer_ref, inner_ref, out_ref, coef_ref):
    coefficients(noise_ref, flow(where_ref, own_inner_ref, own_outer_ref, inner_ref, outer_ref), coef_ref)
    substeps(extended(where_ref, own_outer_ref, inner_ref, outer_ref), coef_ref, out_ref)


def transport_sent(*args):
    return pl.pallas_call(
        sent_kernel,
        out_shape=(
            jax.ShapeDtypeStruct((HALF, X, NZ, NY), jnp.float32),
            jax.ShapeDtypeStruct((len(SLOT), 7, NZ, NY), jnp.float32),
        ),
        in_specs=[SMEM, SMEM] + [VMEM] * 4,
        out_specs=(VMEM, VMEM),
        compiler_params=LIMIT,
        name="transport_sent",
    )(*args)


def kept_kernel(where_ref, own_ref, inner_ref, outer_ref, coef_ref, out_ref):
    substeps(extended(where_ref, own_ref, inner_ref, outer_ref), coef_ref, out_ref)


def transport_kept(where, own, inner, outer, coef):
    return pl.pallas_call(
        kept_kernel,
        out_shape=jax.ShapeDtypeStruct((HALF, X, NZ, NY), jnp.float32),
        in_specs=[SMEM, VMEM, VMEM, VMEM, VMEM],
        out_specs=VMEM,
        compiler_params=LIMIT,
        name="transport_kept",
    )(where, own, inner, outer, coef)


def halves(x):
    hi = x.astype(jnp.bfloat16)
    return hi, (x - hi.astype(jnp.float32)).astype(jnp.bfloat16)


def product(weights, values):
    whi, wlo = weights
    vhi, vlo = halves(values)
    return lax.dot_general(
        jnp.concatenate([whi, whi, wlo], 0),
        jnp.concatenate([vhi, vlo, vhi], 0),
        (((0,), (0,)), ((), ())),
        preferred_element_type=jnp.float32,
    )


ROWS = 32
TILE = 8


def react_kernel(
    where_ref, sent_ref, kept_ref, mine_ref, other_ref, rate_ref, vapour_ref, rate_matrix_ref, stoich_ref, out_ref
):
    cells = X * NZ
    drive_weights = halves(rate_matrix_ref[...])
    source_weights = halves(stoich_ref[...])
    first = where_ref[0] == 0
    fuel = lax.broadcasted_iota(jnp.int32, (S, NY), 0) == 0

    def by_row(ref, row):
        return jnp.swapaxes(jnp.stack([ref[pl.ds(s * cells + row, TILE), :] for s in range(HALF)]), 0, 1)

    for block in range(0, cells, ROWS):
        mixed = []
        for row in range(block, block + ROWS, TILE):
            tiles = [by_row(ref, row) for ref in (sent_ref, kept_ref, mine_ref, other_ref)]
            for j in range(TILE):
                sent, kept, mine, other = (tile[j] for tile in tiles)
                rate = 0.5 * rate_ref[pl.ds(row + j, 1), :]
                vapour = vapour_ref[pl.ds(row + j, 1), :]
                kept = kept - rate * (kept - mine)
                sent = sent - rate * (sent - other)
                both = jnp.concatenate([jnp.where(first, kept, sent), jnp.where(first, sent, kept)], 0)
                mixed.append(both + jnp.where(fuel, vapour, 0.0))
        mixed = jnp.concatenate(mixed, 1)
        speed = jnp.exp(2.0 * jnp.tanh(product(drive_weights, mixed)))
        updated = mixed + product(source_weights, speed)
        for half in range(0, S, HALF):
            for row in range(0, ROWS, TILE):
                tile = [updated[half : half + HALF, (row + j) * NY : (row + j + 1) * NY] for j in range(TILE)]
                tile = jnp.swapaxes(jnp.stack(tile), 0, 1)
                for s in range(HALF):
                    out_ref[pl.ds((half + s) * cells + block + row, TILE), :] = tile[s]


def react(where, sent, kept, mine, other, rates, vapour, rate_matrix, stoich, prefactor):
    rows = X * NZ
    return pl.pallas_call(
        react_kernel,
        out_shape=jax.ShapeDtypeStruct((S * rows, NY), jnp.float32),
        in_specs=[SMEM] + [VMEM] * 8,
        out_specs=VMEM,
        compiler_params=LIMIT,
        name="react",
    )(
        where,
        *(x.reshape(HALF * rows, NY) for x in (sent, kept, mine, other)),
        rates.reshape(rows, NY),
        vapour.reshape(rows, NY),
        rate_matrix.T,
        (stoich * prefactor[None]).T,
    )


def per_device(fields, velocity, diffusivity, noise, mix_rate, evaporation, rate_matrix, stoich, prefactor):
    slabs = lax.axis_size("slab")
    where = jnp.stack([lax.axis_index("field_2"), lax.axis_index("slab")]).astype(jnp.int32)
    inner = [(i, i ^ 1) for i in range(slabs)]
    outer = [(i, i + 1 if i % 2 else i - 1) for i in range(1, slabs - 1)]
    to_outer, to_inner, keep = pack(where, fields, velocity, diffusivity)
    from_outer = lax.ppermute(to_outer, "slab", outer)
    from_inner = lax.ppermute(to_inner, "slab", inner)
    keep_inner = lax.ppermute(keep, "slab", inner)
    keep_outer = lax.ppermute(keep, "slab", outer)
    swap = functools.partial(lax.ppermute, axis_name="field_2", perm=[(0, 1), (1, 0)])
    sent, coef = transport_sent(where, noise[0], to_outer, to_inner, from_outer, from_inner)
    other = swap(sent)
    kept = transport_kept(where, keep, keep_inner, keep_outer, coef)
    chips = lax.axis_size(CHIPS)
    pair = (kept + other).reshape(chips, -1, NZ, NY)
    parts = lax.all_to_all(pair, CHIPS, 0, 0, tiled=True)
    average = jnp.sum(parts, 0) / F
    spread = jnp.broadcast_to(average[None], pair.shape)
    mine = lax.all_to_all(spread, CHIPS, 0, 0, tiled=True)
    updated = react(where, sent, kept, mine, swap(mine), mix_rate, evaporation, rate_matrix, stoich, prefactor)
    return updated.reshape(fields.shape)


def solution(mesh):
    split = Mesh(mesh.devices.reshape(4, 4, 2, mesh.shape["slab"]), (*FIELD, "slab"))
    return jax.shard_map(
        per_device,
        mesh=split,
        in_specs=(
            P(FIELD, None, "slab", None, None),
            P(None, "slab", None, None),
            P("slab", None, None),
            P(FIELD, None, None),
            P("slab", None, None),
            P("slab", None, None),
            P(),
            P(),
            P(),
        ),
        out_specs=P(FIELD, None, "slab", None, None),
        check_vma=False,
    )
```

```python
import functools

import jax
import jax.numpy as jnp
from jax import lax
from jax.experimental import pallas as pl
from jax.experimental.pallas import tpu as pltpu
from jax.sharding import Mesh
from jax.sharding import PartitionSpec as P

F = 32
S = 16
R = 32
SUBSTEPS = 4
X = 4
NZ = 16
NY = 128
HALF = S // 2
CHIPS = ("field_0", "field_1")
FIELD = ("field_0", "field_1", "field_2")


SLOT = {}
for _i in range(1, 3 * X - 1):
    for _k in range(SUBSTEPS):
        if _k < _i < 3 * X - 1 - _k:
            SLOT[_k, _i] = len(SLOT)
TOGETHER = 8
VMEM = pl.BlockSpec(memory_space=pltpu.VMEM)
SMEM = pl.BlockSpec(memory_space=pltpu.SMEM)
LIMIT = pltpu.CompilerParams(vmem_limit_bytes=48 * 2**20)


USED = X - 1
CELLS = X * HALF


def pack_kernel(where_ref, fields_ref, velocity_ref, diffusivity_ref, outer_ref, inner_ref, kept_ref, sems):
    core, odd = where_ref[0], where_ref[1] % 2
    copies = []

    def copy(source, target):
        copies.append(pltpu.make_async_copy(source, target, sems.at[len(copies)]))
        copies[-1].start()

    for target, first, head in (
        (outer_ref, (1 - core) * HALF, odd),
        (inner_ref, (1 - core) * HALF, 1 - odd),
        (kept_ref, core * HALF, None),
    ):
        for j in range(X):
            copy(fields_ref.at[0, pl.ds(first, HALF), j], target.at[pl.ds(j * HALF, HALF)])
        if head is None:
            continue
        for n in range(4):
            source = velocity_ref.at[n] if n < 3 else diffusivity_ref
            copy(source.at[pl.ds(head, USED)], target.at[pl.ds(CELLS + n * USED, USED)])
    for c in copies:
        c.wait()


def pack(where, *arrays):
    planes = (CELLS + 4 * USED, CELLS + 4 * USED, CELLS)
    return pl.pallas_call(
        pack_kernel,
        out_shape=tuple(jax.ShapeDtypeStruct((n, NZ, NY), jnp.float32) for n in planes),
        in_specs=[SMEM] + [pl.BlockSpec(memory_space=pltpu.HBM)] * 3,
        out_specs=(VMEM,) * 3,
        scratch_shapes=[pltpu.SemaphoreType.DMA((3 * X + 8,))],
        compiler_params=LIMIT,
        name="pack",
    )(where, *(pltpu.with_memory_space_constraint(x, pltpu.HBM) for x in arrays))


def extended(where_ref, own_ref, inner_ref, outer_ref):
    odd = where_ref[1] % 2 == 1

    def layer(some, i):
        at = pl.ds(i % X * HALF + some * TOGETHER, TOGETHER)
        if X <= i < 2 * X:
            return own_ref[at]
        inner, outer = inner_ref[at], outer_ref[at]
        return jnp.where(odd, inner, outer) if i < X else jnp.where(odd, outer, inner)

    return layer


def flow(where_ref, own_inner_ref, own_outer_ref, inner_ref, outer_ref):
    odd = where_ref[1] % 2 == 1

    def layer(channel, i):
        def pick(if_odd, if_even, j):
            at = CELLS + channel * USED + j
            return jnp.where(odd, if_odd[at], if_even[at])

        if i < X:
            return pick(inner_ref, outer_ref, i - 1)
        if i >= 2 * X:
            return pick(outer_ref, inner_ref, i - 2 * X)
        if i == X:
            return pick(own_inner_ref, own_outer_ref, 0)
        return pick(own_outer_ref, own_inner_ref, i - X - 1)

    return layer


def coefficients(noise_ref, layer, coef_ref):
    for i in range(1, 3 * X - 1):
        vx, vy, vz, diff = (layer(n, i) for n in range(4))
        stir = jnp.sqrt(2.0 * diff)
        center = 1.0 - 6.0 * diff
        for k in range(SUBSTEPS):
            if (k, i) not in SLOT:
                continue
            hx = 0.5 * (vx - stir * noise_ref[k, 0])
            hy = 0.5 * (vy - stir * noise_ref[k, 1])
            hz = 0.5 * (vz - stir * noise_ref[k, 2])
            for n, c in enumerate((center, diff - hx, diff + hx, diff - hy, diff + hy, diff - hz, diff + hz)):
                coef_ref[SLOT[k, i], n] = c


def substeps(layer, coef_ref, out_ref):
    def some(g, carry):
        scalars = pl.ds(g * TOGETHER, TOGETHER)
        state = [layer(g, i) for i in range(3 * X)]
        for k in range(SUBSTEPS):
            new = [None] * (3 * X)
            for i in range(k + 1, 3 * X - 1 - k):
                c = coef_ref.at[SLOT[k, i]]
                mid = state[i]
                new[i] = (
                    (c[0][None] * mid + c[1][None] * state[i + 1] + c[2][None] * state[i - 1])
                    + (c[3][None] * pltpu.roll(mid, NY - 1, 2) + c[4][None] * pltpu.roll(mid, 1, 2))
                    + (c[5][None] * pltpu.roll(mid, NZ - 1, 1) + c[6][None] * pltpu.roll(mid, 1, 1))
                )
            state = new
        for j in range(X):
            out_ref[scalars, j] = state[X + j]
        return carry

    lax.fori_loop(0, HALF // TOGETHER, some, 0)


def sent_kernel(where_ref, noise_ref, own_outer_ref, own_inner_ref, outer_ref, inner_ref, out_ref, coef_ref):
    coefficients(noise_ref, flow(where_ref, own_inner_ref, own_outer_ref, inner_ref, outer_ref), coef_ref)
    substeps(extended(where_ref, own_outer_ref, inner_ref, outer_ref), coef_ref, out_ref)


def transport_sent(*args):
    return pl.pallas_call(
        sent_kernel,
        out_shape=(
            jax.ShapeDtypeStruct((HALF, X, NZ, NY), jnp.float32),
            jax.ShapeDtypeStruct((len(SLOT), 7, NZ, NY), jnp.float32),
        ),
        in_specs=[SMEM, SMEM] + [VMEM] * 4,
        out_specs=(VMEM, VMEM),
        compiler_params=LIMIT,
        name="transport_sent",
    )(*args)


def kept_kernel(where_ref, own_ref, inner_ref, outer_ref, coef_ref, out_ref):
    substeps(extended(where_ref, own_ref, inner_ref, outer_ref), coef_ref, out_ref)


def transport_kept(where, own, inner, outer, coef):
    return pl.pallas_call(
        kept_kernel,
        out_shape=jax.ShapeDtypeStruct((HALF, X, NZ, NY), jnp.float32),
        in_specs=[SMEM, VMEM, VMEM, VMEM, VMEM],
        out_specs=VMEM,
        compiler_params=LIMIT,
        name="transport_kept",
    )(where, own, inner, outer, coef)


def halves(x):
    hi = x.astype(jnp.bfloat16)
    return hi, (x - hi.astype(jnp.float32)).astype(jnp.bfloat16)


def product(weights, values):
    whi, wlo = weights
    vhi, vlo = halves(values)
    return lax.dot_general(
        jnp.concatenate([whi, whi, wlo], 0),
        jnp.concatenate([vhi, vlo, vhi], 0),
        (((0,), (0,)), ((), ())),
        preferred_element_type=jnp.float32,
    )


ROWS = 32
TILE = 8


def by_row(ref, row):
    return jnp.swapaxes(jnp.stack([ref[pl.ds(s * X * NZ + row, TILE), :] for s in range(HALF)]), 0, 1)


def mix_kernel(sent_ref, kept_ref, mine_ref, rate_ref, rows_ref, mixed_ref):
    for row in range(0, X * NZ, TILE):
        rows_ref[pl.ds(row, TILE)] = by_row(sent_ref, row)
        kept, mine = by_row(kept_ref, row), by_row(mine_ref, row)
        rate = 0.5 * rate_ref[pl.ds(row, TILE), :]
        mixed_ref[pl.ds(row, TILE)] = kept - rate[:, None] * (kept - mine)


def react_kernel(where_ref, sent_ref, kept_ref, other_ref, rate_ref, vapour_ref, rate_matrix_ref, stoich_ref, out_ref):
    cells = X * NZ
    drive_weights = halves(rate_matrix_ref[...])
    source_weights = halves(stoich_ref[...])
    first = where_ref[0] == 0
    fuel = lax.broadcasted_iota(jnp.int32, (S, NY), 0) == 0

    for block in range(0, cells, ROWS):
        mixed = []
        for row in range(block, block + ROWS, TILE):
            others = by_row(other_ref, row)
            for j in range(TILE):
                sent, kept, other = sent_ref[row + j], kept_ref[row + j], others[j]
                rate = 0.5 * rate_ref[pl.ds(row + j, 1), :]
                vapour = vapour_ref[pl.ds(row + j, 1), :]
                sent = sent - rate * (sent - other)
                both = jnp.concatenate([jnp.where(first, kept, sent), jnp.where(first, sent, kept)], 0)
                mixed.append(both + jnp.where(fuel, vapour, 0.0))
        mixed = jnp.concatenate(mixed, 1)
        speed = jnp.exp(2.0 * jnp.tanh(product(drive_weights, mixed)))
        updated = mixed + product(source_weights, speed)
        for half in range(0, S, HALF):
            for row in range(0, ROWS, TILE):
                tile = [updated[half : half + HALF, (row + j) * NY : (row + j + 1) * NY] for j in range(TILE)]
                tile = jnp.swapaxes(jnp.stack(tile), 0, 1)
                for s in range(HALF):
                    out_ref[pl.ds((half + s) * cells + block + row, TILE), :] = tile[s]


def react(where, sent, kept, mine, swap, rates, vapour, rate_matrix, stoich, prefactor):
    rows = X * NZ
    rates = rates.reshape(rows, NY)
    by_rows = jax.ShapeDtypeStruct((rows, HALF, NY), jnp.float32)
    other = swap(mine)
    sent, mixed = pl.pallas_call(
        mix_kernel,
        out_shape=(by_rows, by_rows),
        in_specs=[VMEM] * 4,
        out_specs=(VMEM, VMEM),
        compiler_params=LIMIT,
        name="mix",
    )(*(x.reshape(HALF * rows, NY) for x in (sent, kept, mine)), rates)
    return pl.pallas_call(
        react_kernel,
        out_shape=jax.ShapeDtypeStruct((S * rows, NY), jnp.float32),
        in_specs=[SMEM] + [VMEM] * 7,
        out_specs=VMEM,
        compiler_params=LIMIT,
        name="react",
    )(
        where,
        sent,
        mixed,
        other.reshape(HALF * rows, NY),
        rates,
        vapour.reshape(rows, NY),
        rate_matrix.T,
        (stoich * prefactor[None]).T,
    )


def per_device(fields, velocity, diffusivity, noise, mix_rate, evaporation, rate_matrix, stoich, prefactor):
    slabs = lax.axis_size("slab")
    where = jnp.stack([lax.axis_index("field_2"), lax.axis_index("slab")]).astype(jnp.int32)
    inner = [(i, i ^ 1) for i in range(slabs)]
    outer = [(i, i + 1 if i % 2 else i - 1) for i in range(1, slabs - 1)]
    to_outer, to_inner, keep = pack(where, fields, velocity, diffusivity)
    from_outer = lax.ppermute(to_outer, "slab", outer)
    from_inner = lax.ppermute(to_inner, "slab", inner)
    keep_inner = lax.ppermute(keep, "slab", inner)
    keep_outer = lax.ppermute(keep, "slab", outer)
    swap = functools.partial(lax.ppermute, axis_name="field_2", perm=[(0, 1), (1, 0)])
    sent, coef = transport_sent(where, noise[0], to_outer, to_inner, from_outer, from_inner)
    other = swap(sent)
    kept = transport_kept(where, keep, keep_inner, keep_outer, coef)
    chips = lax.axis_size(CHIPS)
    pair = (kept + other).reshape(chips, -1, NZ, NY)
    parts = lax.all_to_all(pair, CHIPS, 0, 0, tiled=True)
    average = jnp.sum(parts, 0) / F
    spread = jnp.broadcast_to(average[None], pair.shape)
    mine = lax.all_to_all(spread, CHIPS, 0, 0, tiled=True)
    updated = react(where, sent, kept, mine, swap, mix_rate, evaporation, rate_matrix, stoich, prefactor)
    return updated.reshape(fields.shape)


def solution(mesh):
    split = Mesh(mesh.devices.reshape(4, 4, 2, mesh.shape["slab"]), (*FIELD, "slab"))
    return jax.shard_map(
        per_device,
        mesh=split,
        in_specs=(
            P(FIELD, None, "slab", None, None),
            P(None, "slab", None, None),
            P("slab", None, None),
            P(FIELD, None, None),
            P("slab", None, None),
            P("slab", None, None),
            P(),
            P(),
            P(),
        ),
        out_specs=P(FIELD, None, "slab", None, None),
        check_vma=False,
    )
```

```python
import functools

import jax
import jax.numpy as jnp
from jax import lax
from jax.experimental import pallas as pl
from jax.experimental.pallas import tpu as pltpu
from jax.sharding import Mesh
from jax.sharding import PartitionSpec as P

F = 32
S = 16
R = 32
SUBSTEPS = 4
X = 4
NZ = 16
NY = 128
HALF = S // 2
CHIPS = ("field_0", "field_1")
FIELD = ("field_0", "field_1", "field_2")


SLOT = {}
for _i in range(1, 3 * X - 1):
    for _k in range(SUBSTEPS):
        if _k < _i < 3 * X - 1 - _k:
            SLOT[_k, _i] = len(SLOT)
TOGETHER = 8
VMEM = pl.BlockSpec(memory_space=pltpu.VMEM)
SMEM = pl.BlockSpec(memory_space=pltpu.SMEM)
LIMIT = pltpu.CompilerParams(vmem_limit_bytes=48 * 2**20)


USED = X - 1
CELLS = X * HALF


def pack_kernel(where_ref, fields_ref, velocity_ref, diffusivity_ref, outer_ref, inner_ref, kept_ref, sems):
    core, odd = where_ref[0], where_ref[1] % 2
    copies = []

    def copy(source, target):
        copies.append(pltpu.make_async_copy(source, target, sems.at[len(copies)]))
        copies[-1].start()

    for target, first, head in (
        (outer_ref, (1 - core) * HALF, odd),
        (inner_ref, (1 - core) * HALF, 1 - odd),
        (kept_ref, core * HALF, None),
    ):
        for j in range(X):
            copy(fields_ref.at[0, pl.ds(first, HALF), j], target.at[pl.ds(j * HALF, HALF)])
        if head is None:
            continue
        for n in range(4):
            source = velocity_ref.at[n] if n < 3 else diffusivity_ref
            copy(source.at[pl.ds(head, USED)], target.at[pl.ds(CELLS + n * USED, USED)])
    for c in copies:
        c.wait()


def pack(where, *arrays):
    planes = (CELLS + 4 * USED, CELLS + 4 * USED, CELLS)
    return pl.pallas_call(
        pack_kernel,
        out_shape=tuple(jax.ShapeDtypeStruct((n, NZ, NY), jnp.float32) for n in planes),
        in_specs=[SMEM] + [pl.BlockSpec(memory_space=pltpu.HBM)] * 3,
        out_specs=(VMEM,) * 3,
        scratch_shapes=[pltpu.SemaphoreType.DMA((3 * X + 8,))],
        compiler_params=LIMIT,
        name="pack",
    )(where, *(pltpu.with_memory_space_constraint(x, pltpu.HBM) for x in arrays))


def extended(where_ref, own_ref, inner_ref, outer_ref):
    odd = where_ref[1] % 2 == 1

    def layer(some, i):
        at = pl.ds(i % X * HALF + some * TOGETHER, TOGETHER)
        if X <= i < 2 * X:
            return own_ref[at]
        inner, outer = inner_ref[at], outer_ref[at]
        return jnp.where(odd, inner, outer) if i < X else jnp.where(odd, outer, inner)

    return layer


def flow(where_ref, own_inner_ref, own_outer_ref, inner_ref, outer_ref):
    odd = where_ref[1] % 2 == 1

    def layer(channel, i):
        def pick(if_odd, if_even, j):
            at = CELLS + channel * USED + j
            return jnp.where(odd, if_odd[at], if_even[at])

        if i < X:
            return pick(inner_ref, outer_ref, i - 1)
        if i >= 2 * X:
            return pick(outer_ref, inner_ref, i - 2 * X)
        if i == X:
            return pick(own_inner_ref, own_outer_ref, 0)
        return pick(own_outer_ref, own_inner_ref, i - X - 1)

    return layer


def coefficients(noise_ref, layer, coef_ref):
    for i in range(1, 3 * X - 1):
        vx, vy, vz, diff = (layer(n, i) for n in range(4))
        stir = jnp.sqrt(2.0 * diff)
        center = 1.0 - 6.0 * diff
        for k in range(SUBSTEPS):
            if (k, i) not in SLOT:
                continue
            hx = 0.5 * (vx - stir * noise_ref[k, 0])
            hy = 0.5 * (vy - stir * noise_ref[k, 1])
            hz = 0.5 * (vz - stir * noise_ref[k, 2])
            for n, c in enumerate((center, diff - hx, diff + hx, diff - hy, diff + hy, diff - hz, diff + hz)):
                coef_ref[SLOT[k, i], n] = c


def substeps(layer, coef_ref, out_ref):
    def some(g, carry):
        scalars = pl.ds(g * TOGETHER, TOGETHER)
        state = [layer(g, i) for i in range(3 * X)]
        for k in range(SUBSTEPS):
            new = [None] * (3 * X)
            for i in range(k + 1, 3 * X - 1 - k):
                c = coef_ref.at[SLOT[k, i]]
                mid = state[i]
                new[i] = (
                    (c[0][None] * mid + c[1][None] * state[i + 1] + c[2][None] * state[i - 1])
                    + (c[3][None] * pltpu.roll(mid, NY - 1, 2) + c[4][None] * pltpu.roll(mid, 1, 2))
                    + (c[5][None] * pltpu.roll(mid, NZ - 1, 1) + c[6][None] * pltpu.roll(mid, 1, 1))
                )
            state = new
        for j in range(X):
            out_ref[scalars, j] = state[X + j]
        return carry

    lax.fori_loop(0, HALF // TOGETHER, some, 0)


def sent_kernel(where_ref, noise_ref, own_outer_ref, own_inner_ref, outer_ref, inner_ref, out_ref, coef_ref):
    coefficients(noise_ref, flow(where_ref, own_inner_ref, own_outer_ref, inner_ref, outer_ref), coef_ref)
    substeps(extended(where_ref, own_outer_ref, inner_ref, outer_ref), coef_ref, out_ref)


def transport_sent(*args):
    return pl.pallas_call(
        sent_kernel,
        out_shape=(
            jax.ShapeDtypeStruct((HALF, X, NZ, NY), jnp.float32),
            jax.ShapeDtypeStruct((len(SLOT), 7, NZ, NY), jnp.float32),
        ),
        in_specs=[SMEM, SMEM] + [VMEM] * 4,
        out_specs=(VMEM, VMEM),
        compiler_params=LIMIT,
        name="transport_sent",
    )(*args)


def kept_kernel(where_ref, own_ref, inner_ref, outer_ref, coef_ref, out_ref):
    substeps(extended(where_ref, own_ref, inner_ref, outer_ref), coef_ref, out_ref)


def transport_kept(where, own, inner, outer, coef):
    return pl.pallas_call(
        kept_kernel,
        out_shape=jax.ShapeDtypeStruct((HALF, X, NZ, NY), jnp.float32),
        in_specs=[SMEM, VMEM, VMEM, VMEM, VMEM],
        out_specs=VMEM,
        compiler_params=LIMIT,
        name="transport_kept",
    )(where, own, inner, outer, coef)


def halves(x):
    hi = x.astype(jnp.bfloat16)
    return hi, (x - hi.astype(jnp.float32)).astype(jnp.bfloat16)


def product(weights, values):
    whi, wlo = weights
    vhi, vlo = halves(values)
    return lax.dot_general(
        jnp.concatenate([whi, whi, wlo], 0),
        jnp.concatenate([vhi, vlo, vhi], 0),
        (((0,), (0,)), ((), ())),
        preferred_element_type=jnp.float32,
    )


ROWS = 64
TILE = 8


def by_row(ref, row):
    return jnp.swapaxes(jnp.stack([ref[pl.ds(s * X * NZ + row, TILE), :] for s in range(HALF)]), 0, 1)


def mix_kernel(sent_ref, kept_ref, mine_ref, rate_ref, rows_ref, mixed_ref):
    for row in range(0, X * NZ, TILE):
        rows_ref[pl.ds(row, TILE)] = by_row(sent_ref, row)
        kept, mine = by_row(kept_ref, row), by_row(mine_ref, row)
        rate = 0.5 * rate_ref[pl.ds(row, TILE), :]
        mixed_ref[pl.ds(row, TILE)] = kept - rate[:, None] * (kept - mine)


def react_kernel(where_ref, sent_ref, kept_ref, other_ref, rate_ref, vapour_ref, rate_matrix_ref, stoich_ref, out_ref):
    cells = X * NZ
    drive_weights = halves(rate_matrix_ref[...])
    source_weights = halves(stoich_ref[...])
    first = where_ref[0] == 0
    fuel = lax.broadcasted_iota(jnp.int32, (S, NY), 0) == 0

    for block in range(0, cells, ROWS):
        mixed = []
        for row in range(block, block + ROWS, TILE):
            others = by_row(other_ref, row)
            for j in range(TILE):
                sent, kept, other = sent_ref[row + j], kept_ref[row + j], others[j]
                rate = 0.5 * rate_ref[pl.ds(row + j, 1), :]
                vapour = vapour_ref[pl.ds(row + j, 1), :]
                sent = sent - rate * (sent - other)
                both = jnp.concatenate([jnp.where(first, kept, sent), jnp.where(first, sent, kept)], 0)
                mixed.append(both + jnp.where(fuel, vapour, 0.0))
        mixed = jnp.concatenate(mixed, 1)
        speed = jnp.exp(2.0 * jnp.tanh(product(drive_weights, mixed)))
        updated = mixed + product(source_weights, speed)
        for half in range(0, S, HALF):
            for row in range(0, ROWS, TILE):
                tile = [updated[half : half + HALF, (row + j) * NY : (row + j + 1) * NY] for j in range(TILE)]
                tile = jnp.swapaxes(jnp.stack(tile), 0, 1)
                for s in range(HALF):
                    out_ref[pl.ds((half + s) * cells + block + row, TILE), :] = tile[s]


def react(where, sent, kept, mine, swap, rates, vapour, rate_matrix, stoich, prefactor):
    rows = X * NZ
    rates = rates.reshape(rows, NY)
    by_rows = jax.ShapeDtypeStruct((rows, HALF, NY), jnp.float32)
    other = swap(mine)
    sent, mixed = pl.pallas_call(
        mix_kernel,
        out_shape=(by_rows, by_rows),
        in_specs=[VMEM] * 4,
        out_specs=(VMEM, VMEM),
        compiler_params=LIMIT,
        name="mix",
    )(*(x.reshape(HALF * rows, NY) for x in (sent, kept, mine)), rates)
    return pl.pallas_call(
        react_kernel,
        out_shape=jax.ShapeDtypeStruct((S * rows, NY), jnp.float32),
        in_specs=[SMEM] + [VMEM] * 7,
        out_specs=VMEM,
        compiler_params=LIMIT,
        name="react",
    )(
        where,
        sent,
        mixed,
        other.reshape(HALF * rows, NY),
        rates,
        vapour.reshape(rows, NY),
        rate_matrix.T,
        (stoich * prefactor[None]).T,
    )


def per_device(fields, velocity, diffusivity, noise, mix_rate, evaporation, rate_matrix, stoich, prefactor):
    slabs = lax.axis_size("slab")
    where = jnp.stack([lax.axis_index("field_2"), lax.axis_index("slab")]).astype(jnp.int32)
    inner = [(i, i ^ 1) for i in range(slabs)]
    outer = [(i, i + 1 if i % 2 else i - 1) for i in range(1, slabs - 1)]
    to_outer, to_inner, keep = pack(where, fields, velocity, diffusivity)
    from_outer = lax.ppermute(to_outer, "slab", outer)
    from_inner = lax.ppermute(to_inner, "slab", inner)
    keep_inner = lax.ppermute(keep, "slab", inner)
    keep_outer = lax.ppermute(keep, "slab", outer)
    swap = functools.partial(lax.ppermute, axis_name="field_2", perm=[(0, 1), (1, 0)])
    sent, coef = transport_sent(where, noise[0], to_outer, to_inner, from_outer, from_inner)
    other = swap(sent)
    kept = transport_kept(where, keep, keep_inner, keep_outer, coef)
    chips = lax.axis_size(CHIPS)
    pair = (kept + other).reshape(chips, -1, NZ, NY)
    parts = lax.all_to_all(pair, CHIPS, 0, 0, tiled=True)
    average = jnp.sum(parts, 0) / F
    spread = jnp.broadcast_to(average[None], pair.shape)
    mine = lax.all_to_all(spread, CHIPS, 0, 0, tiled=True)
    updated = react(where, sent, kept, mine, swap, mix_rate, evaporation, rate_matrix, stoich, prefactor)
    return updated.reshape(fields.shape)


def solution(mesh):
    split = Mesh(mesh.devices.reshape(4, 4, 2, mesh.shape["slab"]), (*FIELD, "slab"))
    return jax.shard_map(
        per_device,
        mesh=split,
        in_specs=(
            P(FIELD, None, "slab", None, None),
            P(None, "slab", None, None),
            P("slab", None, None),
            P(FIELD, None, None),
            P("slab", None, None),
            P("slab", None, None),
            P(),
            P(),
            P(),
        ),
        out_specs=P(FIELD, None, "slab", None, None),
        check_vma=False,
    )
```
